256 devices in a mesh: sky: 64 (over x, z, core), band: 4 (over y).
Axes of the slice: x: 4, y: 4, z: 8, core: 2. Of those that a mesh axis runs over, the one named last changes fastest.
Arguments:
- raw_blocks: bfloat16 [168, 1376256], P(None, ('sky', 'band')), may hold values from -6 to 6
- patch_of_block: int32 [8192, 1], P(('sky', 'band')), may hold values from 0 to 63; in each aligned block of 32 rows (0 to 31, 32 to 63, ...) at most 2 rows name the same one
- cell_of_block: int32 [8192], P(('sky', 'band')), may hold values from 0 to 15
- band_of_block: int32 [8192], P(('sky', 'band')), may hold values from 0 to 5
- block_weight: bfloat16 [8192], P(('sky', 'band')), may hold values from 0.25 to 4
- basis_coef: bfloat16 [8192, 3], P(('sky', 'band')), may hold values from 0.25 to 1
- row_basis: float32 [3, 41], replicated, may hold values from -1 to 1
- col_basis: float32 [3, 41], replicated, may hold values from -1 to 1
- band_gain: float32 [6], replicated, may hold values from 0.5 to 2
- filter_taps: float32 [41], replicated, may hold values from -1 to 1
Outputs:
- detection: float32 [64, 512, 512], P('sky', 'band')
The draws below stay inside these ranges and needn't reach their ends.
Inputs may be any that keep to these rules, and one draw needn't show every extreme that they name: `patch_of_block`: of the 32 blocks of one device at most 2 intersect one patch, and on some device exactly 2 do.
All inputs are finite; a program needn't handle non-finite values.
Results may differ from the reference program's by a relative error of at most 0.015.
Values may be sent and summed in bfloat16 or wider, within the bound.
A program may use at most 128 MiB of HBM per device.

```python
import math
import jax
import jax.numpy as jnp
import numpy as np
from jax import lax

B = 128
KT = 41
R = 20
P_SIZE = 168
NBASIS = 3
BANDS = 6
CR = 4
CC = 4
CELLS = 16
BLK_DEV = 32
CAP = 2
BLOCKS = 8192
NPATCH = 64


def plant(result, own_key, smallest, high):
    longest = result.shape.index(max(result.shape))
    spots = []
    for shift in (0, 1):
        where = [jax.random.randint(jax.random.fold_in(own_key, axis), (), 0, length) for axis, length in enumerate(result.shape)]
        where[longest] = (where[longest] + shift) % result.shape[longest]
        spots.append(tuple(where))
    return result.at[spots[0]].set(smallest).at[spots[1]].set(high)


def levels(key, dims, split, least, top_value):
    def one(position, parts):
        draws = jax.random.uniform(jax.random.fold_in(jax.random.fold_in(key, 6), position), (parts,), jnp.float32, least / len(split), top_value / len(split))
        return jnp.repeat(jnp.exp(draws), dims[position] // parts).reshape((-1,) + (1,) * (len(dims) - position - 1))

    gain = one(*split[0])
    for cut in split[1:]:
        gain = gain * one(*cut)
    return gain


def shared_out(rng, own, number, rows, amount, top, reach, lean):
    ranking = jax.random.permutation(rng, amount)
    heavy_load, ordinary = portions_of(amount, rows * top, reach, lean, True), portions_of(amount, rows * top, reach, lean, False)
    places = jnp.arange(amount)

    def named(tallies, turn):
        used = int((tallies > 0).sum())
        fixed = max(1, used // 4)
        moved = fixed + (places - fixed + turn * (used - fixed)) % max(1, amount - fixed)
        return jnp.zeros((amount,), jnp.int32).at[ranking[jnp.where(places < fixed, places, moved)]].set(jnp.asarray(tallies, jnp.int32))

    tallies = jnp.where(number % 4 == 0, named(heavy_load, number // 4), named(ordinary, number - number // 4 - 1))
    mixed = jax.random.permutation(jax.random.fold_in(own, 3), amount)
    donor, sink = mixed[0:amount // 2 * 2:2], mixed[1:amount // 2 * 2:2]
    slack = jnp.minimum(tallies[donor] - 1, reach - tallies[sink]) // 2
    slack = jnp.where((donor == ranking[0]) | (sink == ranking[0]) | (tallies[sink] == 0), 0, jnp.maximum(slack, 0))
    moved = jax.random.randint(jax.random.fold_in(own, 4), (amount // 2,), 0, 1 << 20) % (slack + 1)
    tallies = tallies.at[donor].add(-moved).at[sink].add(moved)
    items = jnp.searchsorted(jnp.cumsum(tallies), jnp.arange(rows * top), side="right").astype(jnp.int32)
    grid = items.reshape(top, rows).T
    grid = grid[jax.random.permutation(jax.random.fold_in(own, 1), rows)]
    turn = jax.random.randint(jax.random.fold_in(own, 2), (rows, 1), 0, top)
    return jnp.take_along_axis(grid, (jnp.arange(top)[None, :] + turn) % top, axis=1)


def portions_of(amount, total, limit, skew, full):
    loads = [(1 << 20) // math.isqrt(grade ** skew) + 1 for grade in range(1, amount + 1)]
    largest = limit if full else min(limit, max(-(-total // amount), total * loads[0] // sum(loads)))
    least = 1 if total - largest >= amount - 1 else 0
    given, rest = [largest] + [least] * (amount - 1), total - largest - least * (amount - 1)
    while rest > 0:
        candidates = [i for i in range(1, amount) if given[i] < largest] or [i for i in range(1, amount) if given[i] < limit]
        whole, budget = sum([loads[i] for i in candidates]), rest
        for i in candidates:
            more = min(limit - given[i], max(1, budget * loads[i] // whole), rest)
            given[i] = given[i] + more
            rest = rest - more
    return np.array(given)


def gaussian(own_key, dims, width, limit, pieces=(), held_as=jnp.bfloat16):
    gain = levels(own_key, dims, pieces, -0.22, 0.18) if pieces else 1.0
    entries = jax.random.normal(own_key, dims, jnp.float32) * width * gain
    return jnp.minimum(jnp.maximum(entries, -limit), limit).astype(held_as)


def setup_inputs(seed: int = 0) -> dict:
    splits = jax.random.split(jax.random.key(seed), 11)
    raw_blocks = gaussian(splits[0], (P_SIZE, BLOCKS * P_SIZE), 1.0, 6.0, ((1, 256),))
    patch_of_block_keys = jax.random.split(jax.random.fold_in(splits[1], 1), BLOCKS // BLK_DEV)
    patch_of_block_turns = jax.random.permutation(jax.random.fold_in(splits[1], 3), BLOCKS // BLK_DEV)
    patch_of_block = jax.vmap(lambda own, number: shared_out(jax.random.fold_in(splits[1], 2), own, number, BLK_DEV, NPATCH, 1, CAP, 2))(patch_of_block_keys, patch_of_block_turns).reshape((BLOCKS, 1))
    cell_of_block = plant(jax.random.randint(splits[2], (BLOCKS,), 0, CELLS), jax.random.fold_in(splits[2], 1), 0, CELLS - 1).astype(jnp.int32)
    band_of_block = plant(jax.random.randint(splits[3], (BLOCKS,), 0, BANDS), jax.random.fold_in(splits[3], 1), 0, BANDS - 1).astype(jnp.int32)
    block_weight = jnp.clip(jnp.exp(math.log(4.0) - 2.7725887 * jax.random.uniform(splits[4], (BLOCKS,), jnp.float32) ** levels(splits[4], (BLOCKS,), ((0, 256),), -0.2, 0.2)), 0.25, 4.0).astype(jnp.bfloat16)
    basis_coef = jnp.clip(0.25 + 0.75 * jax.random.uniform(splits[5], (BLOCKS, NBASIS), jnp.float32) ** levels(splits[5], (BLOCKS, NBASIS), ((0, 256),), -0.2, 0.2), 0.25, 1.0).astype(jnp.bfloat16)
    row_basis = gaussian(splits[6], (NBASIS, KT), KT ** -0.5, 1.0, (), jnp.float32)
    col_basis = gaussian(splits[7], (NBASIS, KT), KT ** -0.5, 1.0, (), jnp.float32)
    band_gain = jnp.clip(jnp.exp(jax.random.uniform(splits[8], (BANDS,), jnp.float32, math.log(0.5), math.log(2.0))), 0.5, 2.0)
    filter_taps = gaussian(splits[9], (KT,), KT ** -0.5, 1.0, (), jnp.float32)
    return {"raw_blocks": raw_blocks, "patch_of_block": patch_of_block, "cell_of_block": cell_of_block, "band_of_block": band_of_block, "block_weight": block_weight, "basis_coef": basis_coef, "row_basis": row_basis, "col_basis": col_basis, "band_gain": band_gain, "filter_taps": filter_taps}


highest = lax.Precision.HIGHEST


def toeplitz(tap_values, rows_out):
    tap_count = tap_values.shape[0]
    period = jnp.concatenate([tap_values, jnp.zeros((rows_out,), tap_values.dtype)])
    flat_row = jnp.tile(period, rows_out)[: rows_out * (rows_out + tap_count - 1)]
    return flat_row.reshape(rows_out, rows_out + tap_count - 1)


def kernel_stack(basis_taps):
    stacked = jnp.stack([toeplitz(basis_taps[k], B) for k in range(NBASIS)])
    return lax.optimization_barrier(stacked.astype(jnp.bfloat16)).astype(jnp.float32)


def match_group(row_kernels, col_kernels, raw_group, coef_group):
    sectioned = jnp.einsum("kip,npq->nkiq", row_kernels, raw_group.astype(jnp.float32), precision=highest)
    sectioned = lax.optimization_barrier(sectioned.astype(jnp.bfloat16)).astype(jnp.float32)
    basis_terms = jnp.einsum("nkiq,kjq->nkij", sectioned, col_kernels, precision=highest)
    return jnp.sum(coef_group.astype(jnp.float32)[:, :, None, None] * basis_terms, axis=1).astype(jnp.bfloat16)


def reference(raw_blocks, patch_of_block, cell_of_block, band_of_block, block_weight, basis_coef, row_basis, col_basis, band_gain, filter_taps):
    row_kernels = kernel_stack(row_basis)
    col_kernels = kernel_stack(col_basis)
    groups = BLOCKS // BLK_DEV
    bin_total = NPATCH * BANDS * CELLS
    target_bin = (patch_of_block[:, 0] * (BANDS * CELLS) + band_of_block * CELLS + cell_of_block).astype(jnp.int32)
    block_major = raw_blocks.reshape(P_SIZE, BLOCKS, P_SIZE).transpose(1, 0, 2)

    def accumulate(totals, inputs):
        raw_group, coef_group, weight_group, bin_group = inputs
        matched = match_group(row_kernels, col_kernels, raw_group, coef_group)
        contrib = matched.astype(jnp.float32) * weight_group.astype(jnp.float32)[:, None, None]
        return totals.at[bin_group].add(contrib), None

    totals, unused = lax.scan(
        accumulate,
        jnp.zeros((bin_total, B, B), jnp.float32),
        (block_major.reshape(groups, BLK_DEV, P_SIZE, P_SIZE), basis_coef.reshape(groups, BLK_DEV, NBASIS),
         block_weight.reshape(groups, BLK_DEV), target_bin.reshape(groups, BLK_DEV)))
    weight_sum = jax.ops.segment_sum(block_weight.astype(jnp.float32), target_bin, num_segments=bin_total)
    grid_shape = (NPATCH, BANDS, CR, CC)
    coadd_image = totals.reshape(grid_shape + (B, B)) / jnp.maximum(weight_sum.reshape(grid_shape), 1.0)[..., None, None]
    combined = jnp.sum(band_gain[None, :, None, None, None, None] * coadd_image, axis=1)
    patch_image = combined.transpose(0, 1, 3, 2, 4).reshape(NPATCH, CR * B, CC * B)
    patch_image = lax.optimization_barrier(patch_image.astype(jnp.bfloat16)).astype(jnp.float32)
    padded = jnp.pad(patch_image, ((0, 0), (R, R), (0, 0)))
    filter_round = lax.optimization_barrier(filter_taps.astype(jnp.bfloat16)).astype(jnp.float32)
    row_filter = toeplitz(filter_round, CR * B)
    col_filter = toeplitz(filter_round, CC * B)[:, R:R + CC * B].T
    smoothed = jnp.einsum("ij,pjx->pix", row_filter, padded, precision=highest)
    smoothed = lax.optimization_barrier(smoothed.astype(jnp.bfloat16)).astype(jnp.float32)
    return jnp.einsum("pix,xl->pil", smoothed, col_filter, precision=highest)
```

```python
import functools

import jax
import jax.numpy as jnp
from jax import lax
from jax.experimental import pallas as pl
from jax.experimental.pallas import tpu as pltpu
from jax.sharding import PartitionSpec as P

B = 128
TAPS = 41
RADIUS = 20
SIDE = 168
NBASIS = 3
BANDS = 6
CR = 4
CC = 4
CELLS = 16
TARGETS = BANDS * CELLS
BLK = 32
CAP = 2
NX, NZ, NC, NY = 4, 8, 2, 4
PLANE = NX * NC * NY
PER_DEST = 2
SLOTS = PER_DEST * CAP
PIECE = 176
MESH = pl.DeviceIdType.MESH
F32 = jnp.float32
BF16 = jnp.bfloat16


def coordinates():
    sky = lax.axis_index("sky")
    core = lax.rem(sky, NC)
    z = lax.rem(lax.div(sky, NC), NZ)
    x = lax.div(sky, NC * NZ)
    return x, z, core, lax.axis_index("band")


def device(x, z, core, y):
    return {"sky": (x * NZ + z) * NC + core, "band": y}


def banded(shape, diagonal, taps, rows):
    distance = diagonal(
        lax.broadcasted_iota(jnp.int32, shape, 0), lax.broadcasted_iota(jnp.int32, shape, 1)
    )

    def step(t, held):
        hit = distance == t
        return tuple(jnp.where(hit, taps(k, t), held[k]) for k in range(rows))

    return lax.fori_loop(0, TAPS, step, tuple(jnp.zeros(shape, F32) for _ in range(rows)))


def match_kernel(
    slot_ref, coef_ref, row_ref, col_ref, raw_ref, out_ref, rowk, colk, sectioned
):
    for part in range(0, B, 32):
        stack = banded((32, 256), lambda i, j: j - i - part, lambda k, t: row_ref[k, t], NBASIS)
        for k in range(NBASIS):
            rowk[k * B + part : k * B + part + 32, :] = stack[k].astype(BF16)
    colk[...] = jnp.zeros_like(colk)
    for part in range(0, 192, 64):
        for shift in range(2):
            stack = banded(
                (64, B),
                lambda u, l: u + part - l - 8 * shift,
                lambda k, t: col_ref[k, t],
                NBASIS,
            )
            for k in range(NBASIS):
                colk[shift, k, B + part : B + part + 64, :] = stack[k].astype(BF16)

    def clear(d, _):
        out_ref[pl.ds(d * SLOTS, SLOTS)] = jnp.zeros((SLOTS, B, B), BF16)
        return 0

    lax.fori_loop(0, PLANE, clear, 0)

    def rows(step, _):
        at = pl.ds(pl.multiple_of(step * 256, 256), 256)
        sectioned[:, at] = jnp.dot(
            rowk[:, :SIDE], raw_ref[:, at], preferred_element_type=F32
        ).astype(BF16)
        return 0

    lax.fori_loop(0, BLK * SIDE // 256, rows, 0)

    def columns(group, _):
        for j in range(16):
            first = j * SIDE // B * B
            offset = j * SIDE - first
            width = 256 if offset + SIDE <= 256 else 384
            shift = offset // 8 % 2
            start = B - offset + 8 * shift
            at = pl.ds(pl.multiple_of(group * (16 * SIDE) + first, B), width)
            block = group * 16 + j
            total = None
            for k in range(NBASIS):
                term = coef_ref[block, k] * jnp.dot(
                    sectioned[k * B : (k + 1) * B, at],
                    colk[shift, k, start : start + width, :],
                    preferred_element_type=F32,
                )
                total = term if total is None else total + term
            out_ref[slot_ref[block]] = total.astype(BF16)
        return 0

    lax.fori_loop(0, BLK // 16, columns, 0)


def match(slot, coef, row_basis, col_basis, raw):
    smem = pl.BlockSpec(memory_space=pltpu.SMEM)
    vmem = pl.BlockSpec(memory_space=pltpu.VMEM)
    return pl.pallas_call(
        match_kernel,
        out_shape=jax.ShapeDtypeStruct((PLANE * SLOTS, B, B), BF16),
        in_specs=[smem, smem, smem, smem, vmem],
        out_specs=vmem,
        scratch_shapes=[
            pltpu.VMEM((NBASIS * B, 256), BF16),
            pltpu.VMEM((2, NBASIS, 512, B), BF16),
            pltpu.VMEM((NBASIS * B, BLK * SIDE), BF16),
        ],
        compiler_params=pltpu.CompilerParams(vmem_limit_bytes=48 * 1024 * 1024),
        name="match",
    )(slot, coef, row_basis, col_basis, raw)


def plane_device(index, z):
    return device(
        lax.div(index, NC * NY), z, lax.rem(lax.div(index, NY), NC), lax.rem(index, NY)
    )


def plane_kernel(out_ref, in_ref, own, send_sem, recv_sem, own_sem):
    x, z, core, y = coordinates()
    me = (x * NC + core) * NY + y
    barrier = pltpu.get_barrier_semaphore()
    for step in range(1, PLANE):
        pl.semaphore_signal(
            barrier,
            inc=1,
            device_id=plane_device(lax.rem(me + step, PLANE), z),
            device_id_type=MESH,
        )
    take = pltpu.make_async_copy(out_ref.at[me], own, own_sem)
    take.start()
    pl.semaphore_wait(barrier, PLANE - 1)
    copies = []
    for step in range(1, PLANE):
        peer = lax.rem(me + step, PLANE)
        copy = pltpu.make_async_remote_copy(
            src_ref=out_ref.at[peer],
            dst_ref=in_ref.at[me],
            send_sem=send_sem.at[step],
            recv_sem=recv_sem.at[step],
            device_id=plane_device(peer, z),
            device_id_type=MESH,
        )
        copy.start()
        copies.append(copy)
    take.wait()
    put = pltpu.make_async_copy(own, in_ref.at[me], own_sem)
    put.start()
    put.wait()
    for copy in copies:
        copy.wait()


def plane_exchange(outgoing):
    hbm = pl.BlockSpec(memory_space=pl.ANY)
    return pl.pallas_call(
        plane_kernel,
        out_shape=jax.ShapeDtypeStruct((PLANE, SLOTS, B, B), BF16),
        in_specs=[hbm],
        out_specs=hbm,
        scratch_shapes=[
            pltpu.VMEM((SLOTS, B, B), BF16),
            pltpu.SemaphoreType.DMA((PLANE,)),
            pltpu.SemaphoreType.DMA((PLANE,)),
            pltpu.SemaphoreType.DMA,
        ],
        compiler_params=pltpu.CompilerParams(collective_id=0, has_side_effects=True),
        name="plane_exchange",
    )(outgoing)


def gather_kernel(cell_ref, scale_ref, in_ref, out_ref, total):
    step = pl.program_id(0)
    per_step = in_ref.shape[0]

    @pl.when(step == 0)
    def _():
        def clear(i, _):
            total[pl.ds(pl.multiple_of(i * 64, 64), 64), :] = jnp.zeros((64, CC * B), F32)
            return 0

        lax.fori_loop(0, PER_DEST * CR * B // 64, clear, 0)

    for d in range(per_step):
        for s in range(SLOTS):
            slot = (step * per_step + d) * SLOTS + s
            cell = cell_ref[slot]

            @pl.when(cell >= 0)
            def _():
                row = pl.multiple_of((s // CAP) * (CR * B) + lax.div(cell, CC) * B, B)
                column = pl.multiple_of(lax.rem(cell, CC) * B, B)
                total[pl.ds(row, B), pl.ds(column, B)] += scale_ref[slot] * in_ref[d, s].astype(F32)

    @pl.when(step == pl.num_programs(0) - 1)
    def _():
        for q in range(PER_DEST):
            base = q * CR * B
            for r in range(CR):
                low, high = r * B - RADIUS, (r + 1) * B + RADIUS
                parts = []
                if low < 0:
                    parts.append(jnp.zeros((RADIUS, CC * B), F32))
                parts.append(total[base + max(low, 0) : base + min(high, CR * B), :])
                if high > CR * B:
                    parts.append(jnp.zeros((RADIUS, CC * B), F32))
                parts.append(jnp.zeros((PIECE - SIDE, CC * B), F32))
                out_ref[q * CR + r] = jnp.concatenate(parts, axis=0).astype(BF16)


def gather_slots(cell, scale, arrived):
    smem = pl.BlockSpec(memory_space=pltpu.SMEM)
    per_step = 4
    return pl.pallas_call(
        gather_kernel,
        grid=(PLANE // per_step,),
        out_shape=jax.ShapeDtypeStruct((PER_DEST * CR, PIECE, CC * B), BF16),
        in_specs=[smem, smem, pl.BlockSpec((per_step, SLOTS, B, B), lambda i: (i, 0, 0, 0))],
        out_specs=pl.BlockSpec((PER_DEST * CR, PIECE, CC * B), lambda i: (0, 0, 0)),
        scratch_shapes=[pltpu.VMEM((PER_DEST * CR * B, CC * B), F32)],
        compiler_params=pltpu.CompilerParams(vmem_limit_bytes=48 * 1024 * 1024),
        name="gather_slots",
    )(cell, scale, arrived)


def detect_kernel(
    taps_ref, piece_ref, out_ref, held, rowf, colf, padded, send_sem, recv_sem, own_sem
):
    x, z, core, y = coordinates()
    barrier = pltpu.get_barrier_semaphore()
    me = z * NY + y
    for step in range(1, NZ * NY):
        other = lax.rem(me + step, NZ * NY)
        pl.semaphore_signal(
            barrier,
            inc=1,
            device_id=device(x, lax.div(other, NY), core, lax.rem(other, NY)),
            device_id_type=MESH,
        )
    pl.semaphore_wait(barrier, NZ * NY - 1)

    def outgoing(q, r):
        return pltpu.make_async_remote_copy(
            src_ref=piece_ref.at[q * CR + r],
            dst_ref=held.at[z],
            send_sem=send_sem.at[q * CR + r],
            recv_sem=recv_sem.at[z],
            device_id=device(x, PER_DEST * y + q, core, r),
            device_id_type=MESH,
        )

    def is_own(q, r):
        return (z == PER_DEST * y + q) & (r == y)

    for q in range(PER_DEST):
        for r in range(CR):

            @pl.when(jnp.logical_not(is_own(q, r)))
            def _():
                outgoing(q, r).start()

            @pl.when(is_own(q, r))
            def _():
                pltpu.make_async_copy(piece_ref.at[q * CR + r], held.at[z], own_sem).start()

    def tap(k, t):
        return taps_ref[t]

    for part in range(0, B, 32):
        rowf[part : part + 32, :] = banded((32, 256), lambda i, j: j - i - part, tap, 1)[0].astype(
            BF16
        )
    for part in range(0, 384, 64):
        colf[part : part + 64, :] = banded(
            (64, B), lambda m, l: m + part - B - l + RADIUS, tap, 1
        )[0].astype(BF16)
    padded[:, :B] = jnp.zeros((B, B), BF16)
    padded[:, B + CC * B :] = jnp.zeros((B, B), BF16)

    own_here = y == lax.div(z, PER_DEST)
    for source in range(NZ):
        mine = own_here & (z == source)

        @pl.when(jnp.logical_not(mine))
        def _():
            pltpu.make_async_remote_copy(
                src_ref=piece_ref.at[0],
                dst_ref=held.at[source],
                send_sem=send_sem.at[0],
                recv_sem=recv_sem.at[source],
                device_id=device(x, source, core, lax.div(z, PER_DEST)),
                device_id_type=MESH,
            ).wait_recv()

        @pl.when(mine)
        def _():
            pltpu.make_async_copy(piece_ref.at[0], held.at[source], own_sem).wait()

    for c in range(CC):
        at = slice(c * B, (c + 1) * B)
        combined = held[0, :, at].astype(F32)
        for source in range(1, NZ):
            combined = combined + held[source, :, at].astype(F32)
        padded[:, B + c * B : 2 * B + c * B] = jnp.dot(
            rowf[:, :PIECE], combined.astype(BF16), preferred_element_type=F32
        ).astype(BF16)
    for c in range(CC):
        out_ref[:, c * B : (c + 1) * B] = jnp.dot(
            padded[:, c * B : c * B + 384], colf[...], preferred_element_type=F32
        )
    for q in range(PER_DEST):
        for r in range(CR):

            @pl.when(jnp.logical_not(is_own(q, r)))
            def _():
                outgoing(q, r).wait_send()


def detect(taps, pieces):
    return pl.pallas_call(
        detect_kernel,
        out_shape=jax.ShapeDtypeStruct((B, CC * B), F32),
        in_specs=[pl.BlockSpec(memory_space=pltpu.SMEM), pl.BlockSpec(memory_space=pl.ANY)],
        out_specs=pl.BlockSpec(memory_space=pltpu.VMEM),
        scratch_shapes=[
            pltpu.VMEM((NZ, PIECE, CC * B), BF16),
            pltpu.VMEM((B, 256), BF16),
            pltpu.VMEM((384, B), BF16),
            pltpu.VMEM((B, (CC + 2) * B), BF16),
            pltpu.SemaphoreType.DMA((PER_DEST * CR,)),
            pltpu.SemaphoreType.DMA((NZ,)),
            pltpu.SemaphoreType.DMA,
        ],
        compiler_params=pltpu.CompilerParams(collective_id=1, has_side_effects=True),
        name="detect",
    )(taps, pieces)


def ranks(patch):
    earlier = jnp.arange(BLK)[None, :] < jnp.arange(BLK)[:, None]
    same = patch[..., :, None] == patch[..., None, :]
    return jnp.sum((same & earlier).astype(jnp.int32), axis=-1)


def local(
    raw_blocks,
    patch_of_block,
    cell_of_block,
    band_of_block,
    block_weight,
    basis_coef,
    row_basis,
    col_basis,
    band_gain,
    filter_taps,
):
    x, z, core, y = coordinates()
    patch = patch_of_block[:, 0]
    own_details = jnp.stack(
        [v.astype(F32) for v in (patch, cell_of_block, band_of_block, block_weight)]
    )
    details = lax.all_gather(own_details, ("sky", "band"), axis=0, tiled=False)
    names = details[:, :3].astype(jnp.int32)
    weights = details[:, 3]

    patch_core = patch % NC
    patch_z = patch // NC % NZ
    patch_x = patch // (NC * NZ)
    dest = (patch_x * NC + patch_core) * NY + patch_z // PER_DEST
    slot = dest * SLOTS + (patch_z % PER_DEST) * CAP + ranks(patch)
    outgoing = match(slot, basis_coef.astype(F32), row_basis, col_basis, raw_blocks)
    arrived = plane_exchange(outgoing.reshape(PLANE, SLOTS, B, B))

    first_patch = (x * NZ + PER_DEST * y) * NC + core
    my_patches = first_patch + NC * jnp.arange(PER_DEST, dtype=jnp.int32)
    every_key = (names[:, 0] * TARGETS + names[:, 2] * CELLS + names[:, 1]).reshape(-1)
    every_weight = weights.reshape(-1)
    bins = (my_patches[:, None] * TARGETS + jnp.arange(TARGETS, dtype=jnp.int32)).reshape(-1)
    weight_sum = jnp.sum(
        jnp.where(every_key[None, :] == bins[:, None], every_weight[None, :], 0.0), axis=1
    )
    gain = jnp.tile(jnp.repeat(band_gain, CELLS), PER_DEST) / jnp.maximum(weight_sum, 1.0)
    near = lax.dynamic_index_in_dim(
        details.reshape(NX, NZ, NC * NY, 4, BLK), z, axis=1, keepdims=False
    ).reshape(PLANE, 4, BLK)
    near_names = near[:, :3].astype(jnp.int32)
    near_patch, near_cell = near_names[:, 0], near_names[:, 1]
    near_key = near_patch * TARGETS + near_names[:, 2] * CELLS + near_cell
    near_gain = jnp.sum(jnp.where(near_key[..., None] == bins, gain, 0.0), axis=-1)
    near_scale = near_gain * near[:, 3]
    near_rank = ranks(near_patch)
    chosen = (near_patch[:, None, None, :] == my_patches[:, None, None]) & (
        near_rank[:, None, None, :] == jnp.arange(CAP, dtype=jnp.int32)[:, None]
    )
    scale = jnp.sum(jnp.where(chosen, near_scale[:, None, None, :], 0.0), axis=-1).reshape(-1)
    cell = jnp.sum(jnp.where(chosen, near_cell[:, None, None, :] + 1, 0), axis=-1).reshape(-1) - 1

    pieces = gather_slots(cell, scale, arrived)
    taps = filter_taps.astype(BF16).astype(F32)
    return detect(taps, pieces)[None]


def solution(mesh):
    return jax.shard_map(
        local,
        mesh=mesh,
        in_specs=(
            P(None, ("sky", "band")),
            P(("sky", "band"), None),
            P(("sky", "band")),
            P(("sky", "band")),
            P(("sky", "band")),
            P(("sky", "band"), None),
            P(),
            P(),
            P(),
            P(),
        ),
        out_specs=P("sky", "band", None),
        check_vma=False,
    )
```

```python
import functools

import jax
import jax.numpy as jnp
from jax import lax
from jax.experimental import pallas as pl
from jax.experimental.pallas import tpu as pltpu
from jax.sharding import PartitionSpec as P

B = 128
TAPS = 41
RADIUS = 20
SIDE = 168
NBASIS = 3
BANDS = 6
CR = 4
CC = 4
CELLS = 16
TARGETS = BANDS * CELLS
BLK = 32
CAP = 2
NX, NZ, NC, NY = 4, 8, 2, 4
PLANE = NX * NC * NY
SLOTS = NZ * CAP
STRIP = B // NY
ROWS = B + 2 * STRIP
MESH = pl.DeviceIdType.MESH
F32 = jnp.float32
BF16 = jnp.bfloat16


def coordinates():
    sky = lax.axis_index("sky")
    core = lax.rem(sky, NC)
    z = lax.rem(lax.div(sky, NC), NZ)
    x = lax.div(sky, NC * NZ)
    return x, z, core, lax.axis_index("band")


def device(x, z, core, y):
    return {"sky": (x * NZ + z) * NC + core, "band": y}


def banded(shape, diagonal, taps, rows):
    distance = diagonal(
        lax.broadcasted_iota(jnp.int32, shape, 0), lax.broadcasted_iota(jnp.int32, shape, 1)
    )

    def step(t, held):
        hit = distance == t
        return tuple(jnp.where(hit, taps(k, t), held[k]) for k in range(rows))

    return lax.fori_loop(0, TAPS, step, tuple(jnp.zeros(shape, F32) for _ in range(rows)))


def match_kernel(
    slot_ref, coef_ref, row_ref, col_ref, raw_ref, out_ref, rowk, colk, sectioned
):
    for part in range(0, B, 32):
        stack = banded((32, 256), lambda i, j: j - i - part, lambda k, t: row_ref[k, t], NBASIS)
        for k in range(NBASIS):
            rowk[k * B + part : k * B + part + 32, :] = stack[k].astype(BF16)
    colk[...] = jnp.zeros_like(colk)
    for part in range(0, 192, 64):
        for shift in range(2):
            stack = banded(
                (64, B),
                lambda u, l: u + part - l - 8 * shift,
                lambda k, t: col_ref[k, t],
                NBASIS,
            )
            for k in range(NBASIS):
                colk[shift, k, B + part : B + part + 64, :] = stack[k].astype(BF16)

    def clear(d, _):
        out_ref[pl.ds(d * SLOTS, SLOTS)] = jnp.zeros((SLOTS, STRIP, B), BF16)
        return 0

    lax.fori_loop(0, PLANE, clear, 0)

    def rows(step, _):
        at = pl.ds(pl.multiple_of(step * 256, 256), 256)
        sectioned[:, at] = jnp.dot(
            rowk[:, :SIDE], raw_ref[:, at], preferred_element_type=F32
        ).astype(BF16)
        return 0

    lax.fori_loop(0, BLK * SIDE // 256, rows, 0)

    def columns(group, _):
        for j in range(16):
            first = j * SIDE // B * B
            offset = j * SIDE - first
            width = 256 if offset + SIDE <= 256 else 384
            shift = offset // 8 % 2
            start = B - offset + 8 * shift
            at = pl.ds(pl.multiple_of(group * (16 * SIDE) + first, B), width)
            block = group * 16 + j
            total = None
            for k in range(NBASIS):
                term = coef_ref[block, k] * jnp.dot(
                    sectioned[k * B : (k + 1) * B, at],
                    colk[shift, k, start : start + width, :],
                    preferred_element_type=F32,
                )
                total = term if total is None else total + term
            slot = slot_ref[block]
            for strip in range(NY):
                out_ref[slot + strip * SLOTS] = total[strip * STRIP : (strip + 1) * STRIP].astype(
                    BF16
                )
        return 0

    lax.fori_loop(0, BLK // 16, columns, 0)


def match(slot, coef, row_basis, col_basis, raw):
    smem = pl.BlockSpec(memory_space=pltpu.SMEM)
    vmem = pl.BlockSpec(memory_space=pltpu.VMEM)
    return pl.pallas_call(
        match_kernel,
        out_shape=jax.ShapeDtypeStruct((PLANE * SLOTS, STRIP, B), BF16),
        in_specs=[smem, smem, smem, smem, vmem],
        out_specs=vmem,
        scratch_shapes=[
            pltpu.VMEM((NBASIS * B, 256), BF16),
            pltpu.VMEM((2, NBASIS, 512, B), BF16),
            pltpu.VMEM((NBASIS * B, BLK * SIDE), BF16),
        ],
        compiler_params=pltpu.CompilerParams(vmem_limit_bytes=24 * 1024 * 1024),
        name="match",
    )(slot, coef, row_basis, col_basis, raw)


def plane_device(index, z):
    return device(
        lax.div(index, NC * NY), z, lax.rem(lax.div(index, NY), NC), lax.rem(index, NY)
    )


def plane_kernel(
    out_ref,
    info_ref,
    in_ref,
    every_ref,
    own,
    send_sem,
    recv_sem,
    info_send,
    info_recv,
    z_send,
    z_recv,
    own_sem,
    info_sem,
):
    x, z, core, y = coordinates()
    me = (x * NC + core) * NY + y
    barrier = pltpu.get_barrier_semaphore()
    for step in range(1, PLANE):
        pl.semaphore_signal(
            barrier,
            inc=1,
            device_id=plane_device(lax.rem(me + step, PLANE), z),
            device_id_type=MESH,
        )
    for step in range(1, NZ):
        pl.semaphore_signal(
            barrier,
            inc=1,
            device_id=device(x, lax.rem(z + step, NZ), core, y),
            device_id_type=MESH,
        )
    take = pltpu.make_async_copy(out_ref.at[me], own, own_sem)
    take.start()
    keep = pltpu.make_async_copy(info_ref.at[0], every_ref.at[z, me], info_sem)
    keep.start()
    pl.semaphore_wait(barrier, PLANE - 1 + NZ - 1)
    infos = []
    for step in range(1, PLANE):
        copy = pltpu.make_async_remote_copy(
            src_ref=info_ref.at[0],
            dst_ref=every_ref.at[z, me],
            send_sem=info_send.at[step],
            recv_sem=info_recv.at[step],
            device_id=plane_device(lax.rem(me + step, PLANE), z),
            device_id_type=MESH,
        )
        copy.start()
        infos.append(copy)
    copies = []
    for step in range(1, PLANE):
        peer = lax.rem(me + step, PLANE)
        copy = pltpu.make_async_remote_copy(
            src_ref=out_ref.at[peer],
            dst_ref=in_ref.at[me],
            send_sem=send_sem.at[step],
            recv_sem=recv_sem.at[step],
            device_id=plane_device(peer, z),
            device_id_type=MESH,
        )
        copy.start()
        copies.append(copy)
    take.wait()
    put = pltpu.make_async_copy(own, in_ref.at[me], own_sem)
    put.start()
    keep.wait()
    for copy in infos:
        copy.wait()
    planes = []
    for step in range(1, NZ):
        copy = pltpu.make_async_remote_copy(
            src_ref=every_ref.at[z],
            dst_ref=every_ref.at[z],
            send_sem=z_send.at[step],
            recv_sem=z_recv.at[step],
            device_id=device(x, lax.rem(z + step, NZ), core, y),
            device_id_type=MESH,
        )
        copy.start()
        planes.append(copy)
    put.wait()
    for copy in planes:
        copy.wait()
    for copy in copies:
        copy.wait()


def plane_exchange(outgoing, info):
    hbm = pl.BlockSpec(memory_space=pl.ANY)
    vmem = pl.BlockSpec(memory_space=pltpu.VMEM)
    dma = pltpu.SemaphoreType.DMA
    return pl.pallas_call(
        plane_kernel,
        out_shape=(
            jax.ShapeDtypeStruct((PLANE, SLOTS, STRIP, B), BF16),
            jax.ShapeDtypeStruct((NZ, PLANE, 1, B), F32),
        ),
        in_specs=[hbm, vmem],
        out_specs=(hbm, vmem),
        scratch_shapes=[
            pltpu.VMEM((SLOTS, STRIP, B), BF16),
            dma((PLANE,)),
            dma((PLANE,)),
            dma((PLANE,)),
            dma((PLANE,)),
            dma((NZ,)),
            dma((NZ,)),
            dma,
            dma,
        ],
        compiler_params=pltpu.CompilerParams(
            collective_id=0, has_side_effects=True, vmem_limit_bytes=4 * 1024 * 1024
        ),
        name="plane_exchange",
    )(outgoing, info)


def gather_kernel(cell_ref, scale_ref, in_ref, out_ref, total):
    step = pl.program_id(0)
    per_step = in_ref.shape[0]

    @pl.when(step == 0)
    def _():
        def clear(i, _):
            total[i] = jnp.zeros((STRIP, CC * B), F32)
            return 0

        lax.fori_loop(0, NZ * CR, clear, 0)

    for d in range(per_step):
        for s in range(SLOTS):
            slot = (step * per_step + d) * SLOTS + s
            cell = cell_ref[slot]

            @pl.when(cell >= 0)
            def _():
                row = (s // CAP) * CR + lax.div(cell, CC)
                column = pl.multiple_of(lax.rem(cell, CC) * B, B)
                total[row, :, pl.ds(column, B)] += scale_ref[slot] * in_ref[d, s].astype(F32)

    @pl.when(step == pl.num_programs(0) - 1)
    def _():
        def write(i, _):
            out_ref[i] = total[i].astype(BF16)
            return 0

        lax.fori_loop(0, NZ * CR, write, 0)


def gather_slots(cell, scale, arrived):
    smem = pl.BlockSpec(memory_space=pltpu.SMEM)
    per_step = 4
    shape = (NZ * CR, STRIP, CC * B)
    return pl.pallas_call(
        gather_kernel,
        grid=(PLANE // per_step,),
        out_shape=jax.ShapeDtypeStruct(shape, BF16),
        in_specs=[smem, smem, pl.BlockSpec((per_step, SLOTS, STRIP, B), lambda i: (i, 0, 0, 0))],
        out_specs=pl.BlockSpec(shape, lambda i: (0, 0, 0)),
        scratch_shapes=[pltpu.VMEM(shape, F32)],
        compiler_params=pltpu.CompilerParams(vmem_limit_bytes=16 * 1024 * 1024),
        name="gather_slots",
    )(cell, scale, arrived)


def detect_kernel(
    taps_ref,
    piece_ref,
    out_ref,
    held,
    strips,
    window,
    rowf,
    colf,
    padded,
    z_send,
    z_recv,
    y_send,
    y_recv,
    edge_send,
    edge_recv,
    own_sem,
):
    x, z, core, y = coordinates()
    barrier = pltpu.get_barrier_semaphore()
    for step in range(1, NZ):
        pl.semaphore_signal(
            barrier,
            inc=1,
            device_id=device(x, lax.rem(z + step, NZ), core, y),
            device_id_type=MESH,
        )
    for step in range(1, NY):
        pl.semaphore_signal(
            barrier,
            inc=1,
            device_id=device(x, z, core, lax.rem(y + step, NY)),
            device_id_type=MESH,
        )
    keep = pltpu.make_async_copy(piece_ref.at[z], held.at[z], own_sem)
    keep.start()
    pl.semaphore_wait(barrier, NZ - 1 + NY - 1)
    pieces = []
    for step in (4, 3, 5, 2, 6, 1, 7):
        peer = lax.rem(z + step, NZ)
        copy = pltpu.make_async_remote_copy(
            src_ref=piece_ref.at[peer],
            dst_ref=held.at[z],
            send_sem=z_send.at[step],
            recv_sem=z_recv.at[step],
            device_id=device(x, peer, core, y),
            device_id_type=MESH,
        )
        copy.start()
        pieces.append(copy)

    def tap(k, t):
        return taps_ref[t]

    for part in range(0, B, 32):
        rowf[part : part + 32, :] = banded(
            (32, 256), lambda i, u: u - i - part - (STRIP - RADIUS), tap, 1
        )[0].astype(BF16)
    for part in range(0, 384, 64):
        colf[part : part + 64, :] = banded(
            (64, B), lambda m, l: m + part - B - l + RADIUS, tap, 1
        )[0].astype(BF16)
    padded[:, :B] = jnp.zeros((B, B), BF16)
    padded[:, B + CC * B :] = jnp.zeros((B, B), BF16)

    keep.wait()
    for copy in pieces:
        copy.wait()
    for r in range(CR):
        combined = held[0, r].astype(F32)
        for source in range(1, NZ):
            combined = combined + held[source, r].astype(F32)
        strips[r] = combined.astype(BF16)

    sends = []
    for step in range(1, NY):
        r = lax.rem(y + step, NY)
        copy = pltpu.make_async_remote_copy(
            src_ref=strips.at[r],
            dst_ref=window.at[1 + y],
            send_sem=y_send.at[step],
            recv_sem=y_recv.at[step],
            device_id=device(x, z, core, r),
            device_id_type=MESH,
        )
        copy.start()
        sends.append(copy)

    def edge(r, upper):
        return pltpu.make_async_remote_copy(
            src_ref=strips.at[r - 1 if upper else r + 1],
            dst_ref=window.at[0 if upper else NY + 1],
            send_sem=edge_send.at[r],
            recv_sem=edge_recv.at[0 if upper else 1],
            device_id=device(x, z, core, r),
            device_id_type=MESH,
        )

    @pl.when(y == NY - 1)
    def _():
        for r in range(1, NY - 1):
            edge(r, True).start()
        window[0] = strips[NY - 2]
        window[NY + 1] = jnp.zeros((STRIP, CC * B), BF16)

    @pl.when(y == 0)
    def _():
        for r in range(1, NY - 1):
            edge(r, False).start()
        window[0] = jnp.zeros((STRIP, CC * B), BF16)
        window[NY + 1] = strips[1]

    window[1 + y] = strips[y]
    for copy in sends:
        copy.wait()

    @pl.when((y > 0) & (y < NY - 1))
    def _():
        edge(1, True).wait_recv()
        edge(1, False).wait_recv()

    @pl.when(y == NY - 1)
    def _():
        for r in range(1, NY - 1):
            edge(r, True).wait_send()

    @pl.when(y == 0)
    def _():
        for r in range(1, NY - 1):
            edge(r, False).wait_send()

    for c in range(CC):
        at = slice(c * B, (c + 1) * B)
        padded[:, B + c * B : 2 * B + c * B] = jnp.dot(
            rowf[:, :ROWS], window[:, :, at].reshape(ROWS, B), preferred_element_type=F32
        ).astype(BF16)
    for c in range(CC):
        out_ref[:, c * B : (c + 1) * B] = jnp.dot(
            padded[:, c * B : c * B + 384], colf[...], preferred_element_type=F32
        )


def detect(taps, pieces):
    dma = pltpu.SemaphoreType.DMA
    return pl.pallas_call(
        detect_kernel,
        out_shape=jax.ShapeDtypeStruct((B, CC * B), F32),
        in_specs=[pl.BlockSpec(memory_space=pltpu.SMEM), pl.BlockSpec(memory_space=pl.ANY)],
        out_specs=pl.BlockSpec(memory_space=pltpu.VMEM),
        scratch_shapes=[
            pltpu.VMEM((NZ, CR, STRIP, CC * B), BF16),
            pltpu.VMEM((CR, STRIP, CC * B), BF16),
            pltpu.VMEM((NY + 2, STRIP, CC * B), BF16),
            pltpu.VMEM((B, 256), BF16),
            pltpu.VMEM((384, B), BF16),
            pltpu.VMEM((B, (CC + 2) * B), BF16),
            dma((NZ,)),
            dma((NZ,)),
            dma((NY,)),
            dma((NY,)),
            dma((NY,)),
            dma((2,)),
            dma,
        ],
        compiler_params=pltpu.CompilerParams(
            collective_id=1, has_side_effects=True, vmem_limit_bytes=8 * 1024 * 1024
        ),
        name="detect",
    )(taps, pieces)


def ranks(patch):
    earlier = jnp.arange(BLK)[None, :] < jnp.arange(BLK)[:, None]
    same = patch[..., :, None] == patch[..., None, :]
    return jnp.sum((same & earlier).astype(jnp.int32), axis=-1)


def local(
    raw_blocks,
    patch_of_block,
    cell_of_block,
    band_of_block,
    block_weight,
    basis_coef,
    row_basis,
    col_basis,
    band_gain,
    filter_taps,
):
    x, z, core, y = coordinates()
    patch = patch_of_block[:, 0]
    own_details = jnp.stack(
        [v.astype(F32) for v in (patch, cell_of_block, band_of_block, block_weight)]
    )
    patch_core = patch % NC
    patch_z = patch // NC % NZ
    patch_x = patch // (NC * NZ)
    slot = (patch_x * NC + patch_core) * (NY * SLOTS) + patch_z * CAP + ranks(patch)
    outgoing = match(slot, basis_coef.astype(F32), row_basis, col_basis, raw_blocks)
    arrived, details = plane_exchange(
        outgoing.reshape(PLANE, SLOTS, STRIP, B), own_details.reshape(1, 1, 4 * BLK)
    )
    details = details.reshape(NZ, PLANE, 4, BLK)

    my_patches = (x * NZ + jnp.arange(NZ, dtype=jnp.int32)) * NC + core
    every_patch = details[:, :, 0].astype(jnp.int32).reshape(-1)
    every_target = (details[:, :, 2] * CELLS + details[:, :, 1]).astype(jnp.int32).reshape(-1)
    every_weight = details[:, :, 3].reshape(-1)
    share = jnp.where(every_patch == my_patches[:, None], every_weight, 0.0).astype(BF16)
    hits = (every_target == jnp.arange(TARGETS, dtype=jnp.int32)[:, None]).astype(BF16)
    weight_sum = lax.dot_general(
        share, hits, (((1,), (1,)), ((), ())), preferred_element_type=F32
    )
    gain = (jnp.repeat(band_gain, CELLS) / jnp.maximum(weight_sum, 1.0)).reshape(-1)
    bins = (my_patches[:, None] * TARGETS + jnp.arange(TARGETS, dtype=jnp.int32)).reshape(-1)
    near = lax.dynamic_index_in_dim(details, z, axis=0, keepdims=False)
    near_names = near[:, :3].astype(jnp.int32)
    near_patch, near_cell = near_names[:, 0], near_names[:, 1]
    near_key = near_patch * TARGETS + near_names[:, 2] * CELLS + near_cell
    near_gain = jnp.sum(jnp.where(near_key[..., None] == bins, gain, 0.0), axis=-1)
    near_scale = near_gain * near[:, 3]
    near_rank = ranks(near_patch)
    chosen = (near_patch[:, None, None, :] == my_patches[:, None, None]) & (
        near_rank[:, None, None, :] == jnp.arange(CAP, dtype=jnp.int32)[:, None]
    )
    scale = jnp.sum(jnp.where(chosen, near_scale[:, None, None, :], 0.0), axis=-1).reshape(-1)
    cell = jnp.sum(jnp.where(chosen, near_cell[:, None, None, :] + 1, 0), axis=-1).reshape(-1) - 1

    pieces = gather_slots(cell, scale, arrived).reshape(NZ, CR, STRIP, CC * B)
    taps = filter_taps.astype(BF16).astype(F32)
    return detect(taps, pieces)[None]


def solution(mesh):
    return jax.shard_map(
        local,
        mesh=mesh,
        in_specs=(
            P(None, ("sky", "band")),
            P(("sky", "band"), None),
            P(("sky", "band")),
            P(("sky", "band")),
            P(("sky", "band")),
            P(("sky", "band"), None),
            P(),
            P(),
            P(),
            P(),
        ),
        out_specs=P("sky", "band", None),
        check_vma=False,
    )
```

```python
import functools

import jax
import jax.numpy as jnp
from jax import lax
from jax.experimental import pallas as pl
from jax.experimental.pallas import tpu as pltpu
from jax.sharding import PartitionSpec as P

B = 128
TAPS = 41
RADIUS = 20
SIDE = 168
NBASIS = 3
BANDS = 6
CR = 4
CC = 4
CELLS = 16
TARGETS = BANDS * CELLS
BLK = 32
CAP = 2
NX, NZ, NC, NY = 4, 8, 2, 4
PLANE = NX * NC * NY
SLOTS = NZ * CAP
STRIP = B // NY
ROWS = B + 2 * STRIP
MESH = pl.DeviceIdType.MESH
HALFWAY = ((2, 2), (2, 0), (0, 2), (2, 1), (1, 2), (2, 3), (3, 2))
RELAYED = tuple((dx, 1, dy) for dx, dy in HALFWAY)
DIRECT = tuple((dx, 0, dy) for dx, dy in HALFWAY) + tuple(
    (dx, dc, dy)
    for dx, dy in ((1, 3), (3, 1), (1, 1), (3, 3), (1, 0), (3, 0), (0, 1), (0, 3), (0, 0))
    for dc in range(NC)
    if (dx, dc, dy) != (0, 0, 0)
)
F32 = jnp.float32
BF16 = jnp.bfloat16


def coordinates():
    sky = lax.axis_index("sky")
    core = lax.rem(sky, NC)
    z = lax.rem(lax.div(sky, NC), NZ)
    x = lax.div(sky, NC * NZ)
    return x, z, core, lax.axis_index("band")


def device(x, z, core, y):
    return {"sky": (x * NZ + z) * NC + core, "band": y}


def banded(shape, diagonal, taps, rows):
    distance = diagonal(
        lax.broadcasted_iota(jnp.int32, shape, 0), lax.broadcasted_iota(jnp.int32, shape, 1)
    )

    def step(t, held):
        hit = distance == t
        return tuple(jnp.where(hit, taps(k, t), held[k]) for k in range(rows))

    return lax.fori_loop(0, TAPS, step, tuple(jnp.zeros(shape, F32) for _ in range(rows)))


def match_kernel(
    slot_ref, coef_ref, row_ref, col_ref, raw_ref, out_ref, rowk, colk, sectioned
):
    for part in range(0, B, 32):
        stack = banded((32, 256), lambda i, j: j - i - part, lambda k, t: row_ref[k, t], NBASIS)
        for k in range(NBASIS):
            rowk[k * B + part : k * B + part + 32, :] = stack[k].astype(BF16)
    colk[...] = jnp.zeros_like(colk)
    for part in range(0, 192, 64):
        for shift in range(2):
            stack = banded(
                (64, B),
                lambda u, l: u + part - l - 8 * shift,
                lambda k, t: col_ref[k, t],
                NBASIS,
            )
            for k in range(NBASIS):
                colk[shift, k, B + part : B + part + 64, :] = stack[k].astype(BF16)

    def clear(d, _):
        out_ref[pl.ds(d * SLOTS, SLOTS)] = jnp.zeros((SLOTS, STRIP, B), BF16)
        return 0

    lax.fori_loop(0, PLANE, clear, 0)

    def rows(step, _):
        at = pl.ds(pl.multiple_of(step * 256, 256), 256)
        sectioned[:, at] = jnp.dot(
            rowk[:, :SIDE], raw_ref[:, at], preferred_element_type=F32
        ).astype(BF16)
        return 0

    lax.fori_loop(0, BLK * SIDE // 256, rows, 0)

    def columns(group, _):
        for j in range(16):
            first = j * SIDE // B * B
            offset = j * SIDE - first
            width = 256 if offset + SIDE <= 256 else 384
            shift = offset // 8 % 2
            start = B - offset + 8 * shift
            at = pl.ds(pl.multiple_of(group * (16 * SIDE) + first, B), width)
            block = group * 16 + j
            total = None
            for k in range(NBASIS):
                term = coef_ref[block, k] * jnp.dot(
                    sectioned[k * B : (k + 1) * B, at],
                    colk[shift, k, start : start + width, :],
                    preferred_element_type=F32,
                )
                total = term if total is None else total + term
            slot = slot_ref[block]
            for strip in range(NY):
                out_ref[slot + strip * SLOTS] = total[strip * STRIP : (strip + 1) * STRIP].astype(
                    BF16
                )
        return 0

    lax.fori_loop(0, BLK // 16, columns, 0)


def match(slot, coef, row_basis, col_basis, raw):
    smem = pl.BlockSpec(memory_space=pltpu.SMEM)
    vmem = pl.BlockSpec(memory_space=pltpu.VMEM)
    return pl.pallas_call(
        match_kernel,
        out_shape=jax.ShapeDtypeStruct((PLANE * SLOTS, STRIP, B), BF16),
        in_specs=[smem, smem, smem, smem, vmem],
        out_specs=vmem,
        scratch_shapes=[
            pltpu.VMEM((NBASIS * B, 256), BF16),
            pltpu.VMEM((2, NBASIS, 512, B), BF16),
            pltpu.VMEM((NBASIS * B, BLK * SIDE), BF16),
        ],
        compiler_params=pltpu.CompilerParams(vmem_limit_bytes=24 * 1024 * 1024),
        name="match",
    )(slot, coef, row_basis, col_basis, raw)


def offset_id(offset):
    dx, dc, dy = offset
    return (dx * NC + dc) * NY + dy


def plane_kernel(
    out_ref,
    info_ref,
    in_ref,
    every_ref,
    own,
    passing,
    send_sem,
    recv_sem,
    pass_send,
    pass_recv,
    info_send,
    info_recv,
    z_send,
    z_recv,
    own_sem,
    info_sem,
):
    x, z, core, y = coordinates()
    me = (x * NC + core) * NY + y

    def moved(dx, dc, dy):
        return lax.rem(x + dx, NX), lax.rem(core + dc, NC), lax.rem(y + dy, NY)

    def index(place):
        return (place[0] * NC + place[1]) * NY + place[2]

    def at(place):
        return device(place[0], z, place[1], place[2])

    everyone = RELAYED + DIRECT
    barrier = pltpu.get_barrier_semaphore()
    for offset in everyone:
        pl.semaphore_signal(barrier, inc=1, device_id=at(moved(*offset)), device_id_type=MESH)
    for step in range(1, NZ):
        pl.semaphore_signal(
            barrier,
            inc=1,
            device_id=device(x, lax.rem(z + step, NZ), core, y),
            device_id_type=MESH,
        )
    take = pltpu.make_async_copy(out_ref.at[me], own, own_sem)
    take.start()
    keep = pltpu.make_async_copy(info_ref.at[0], every_ref.at[z, me], info_sem)
    keep.start()
    pl.semaphore_wait(barrier, PLANE - 1 + NZ - 1)
    infos = []
    for offset in everyone:
        copy = pltpu.make_async_remote_copy(
            src_ref=info_ref.at[0],
            dst_ref=every_ref.at[z, me],
            send_sem=info_send.at[offset_id(offset)],
            recv_sem=info_recv.at[offset_id(offset)],
            device_id=at(moved(*offset)),
            device_id_type=MESH,
        )
        copy.start()
        infos.append(copy)
    firsts = []
    for k, (dx, dc, dy) in enumerate(RELAYED):
        back_x, back_y = (NX - 1) * (dx == 2), (NY - 1) * (dy == 2)
        copy = pltpu.make_async_remote_copy(
            src_ref=out_ref.at[index(moved(dx, dc, dy))],
            dst_ref=passing.at[k],
            send_sem=pass_send.at[k],
            recv_sem=pass_recv.at[k],
            device_id=at(moved(back_x, 0, back_y)),
            device_id_type=MESH,
        )
        copy.start()
        firsts.append(copy)
    copies = []
    for offset in DIRECT:
        copy = pltpu.make_async_remote_copy(
            src_ref=out_ref.at[index(moved(*offset))],
            dst_ref=in_ref.at[me],
            send_sem=send_sem.at[offset_id(offset)],
            recv_sem=recv_sem.at[offset_id(offset)],
            device_id=at(moved(*offset)),
            device_id_type=MESH,
        )
        copy.start()
        copies.append(copy)
    take.wait()
    put = pltpu.make_async_copy(own, in_ref.at[me], own_sem)
    put.start()
    keep.wait()
    for copy in infos:
        copy.wait()
    planes = []
    for step in range(1, NZ):
        copy = pltpu.make_async_remote_copy(
            src_ref=every_ref.at[z],
            dst_ref=every_ref.at[z],
            send_sem=z_send.at[step],
            recv_sem=z_recv.at[step],
            device_id=device(x, lax.rem(z + step, NZ), core, y),
            device_id_type=MESH,
        )
        copy.start()
        planes.append(copy)
    for k, offset in enumerate(RELAYED):
        dx, dc, dy = offset
        ahead_x, ahead_y = dx == 2, dy == 2
        firsts[k].wait_recv()
        copy = pltpu.make_async_remote_copy(
            src_ref=passing.at[k],
            dst_ref=in_ref.at[index(moved(int(ahead_x), 0, int(ahead_y)))],
            send_sem=send_sem.at[offset_id(offset)],
            recv_sem=recv_sem.at[offset_id(offset)],
            device_id=at(moved((dx + ahead_x) % NX, dc, (dy + ahead_y) % NY)),
            device_id_type=MESH,
        )
        copy.start()
        copies.append(copy)
    put.wait()
    for copy in planes:
        copy.wait()
    for copy in firsts:
        copy.wait_send()
    for copy in copies:
        copy.wait()


def plane_exchange(outgoing, info):
    hbm = pl.BlockSpec(memory_space=pl.ANY)
    vmem = pl.BlockSpec(memory_space=pltpu.VMEM)
    dma = pltpu.SemaphoreType.DMA
    return pl.pallas_call(
        plane_kernel,
        out_shape=(
            jax.ShapeDtypeStruct((PLANE, SLOTS, STRIP, B), BF16),
            jax.ShapeDtypeStruct((NZ, PLANE, 1, B), F32),
        ),
        in_specs=[hbm, vmem],
        out_specs=(pl.BlockSpec(memory_space=pltpu.HBM), vmem),
        scratch_shapes=[
            pltpu.VMEM((SLOTS, STRIP, B), BF16),
            pltpu.VMEM((len(RELAYED), SLOTS, STRIP, B), BF16),
            dma((PLANE,)),
            dma((PLANE,)),
            dma((len(RELAYED),)),
            dma((len(RELAYED),)),
            dma((PLANE,)),
            dma((PLANE,)),
            dma((NZ,)),
            dma((NZ,)),
            dma,
            dma,
        ],
        compiler_params=pltpu.CompilerParams(
            collective_id=0, has_side_effects=True, vmem_limit_bytes=4 * 1024 * 1024
        ),
        name="plane_exchange",
    )(outgoing, info)


def gather_kernel(cell_ref, scale_ref, in_ref, out_ref, total):
    step = pl.program_id(0)
    per_step = in_ref.shape[0]

    @pl.when(step == 0)
    def _():
        def clear(i, _):
            total[i] = jnp.zeros((STRIP, CC * B), F32)
            return 0

        lax.fori_loop(0, NZ * CR, clear, 0)

    for d in range(per_step):
        for s in range(SLOTS):
            slot = (step * per_step + d) * SLOTS + s
            cell = cell_ref[slot]

            @pl.when(cell >= 0)
            def _():
                row = (s // CAP) * CR + lax.div(cell, CC)
                column = pl.multiple_of(lax.rem(cell, CC) * B, B)
                total[row, :, pl.ds(column, B)] += scale_ref[slot] * in_ref[d, s].astype(F32)

    @pl.when(step == pl.num_programs(0) - 1)
    def _():
        def write(i, _):
            out_ref[i] = total[i].astype(BF16)
            return 0

        lax.fori_loop(0, NZ * CR, write, 0)


def gather_slots(cell, scale, arrived):
    smem = pl.BlockSpec(memory_space=pltpu.SMEM)
    per_step = 4
    shape = (NZ * CR, STRIP, CC * B)
    return pl.pallas_call(
        gather_kernel,
        grid=(PLANE // per_step,),
        out_shape=jax.ShapeDtypeStruct(shape, BF16),
        in_specs=[smem, smem, pl.BlockSpec((per_step, SLOTS, STRIP, B), lambda i: (i, 0, 0, 0))],
        out_specs=pl.BlockSpec(shape, lambda i: (0, 0, 0)),
        scratch_shapes=[pltpu.VMEM(shape, F32)],
        compiler_params=pltpu.CompilerParams(vmem_limit_bytes=16 * 1024 * 1024),
        name="gather_slots",
    )(cell, scale, arrived)


def detect_kernel(
    taps_ref,
    piece_ref,
    out_ref,
    held,
    passing,
    strips,
    window,
    rowf,
    colf,
    padded,
    z_send,
    z_recv,
    far_send,
    far_recv,
    y_send,
    y_recv,
    edge_send,
    edge_recv,
    own_sem,
):
    x, z, core, y = coordinates()
    barrier = pltpu.get_barrier_semaphore()
    for step in range(1, NZ):
        pl.semaphore_signal(
            barrier,
            inc=1,
            device_id=device(x, lax.rem(z + step, NZ), core, y),
            device_id_type=MESH,
        )
    for step in range(1, NY):
        pl.semaphore_signal(
            barrier,
            inc=1,
            device_id=device(x, z, core, lax.rem(y + step, NY)),
            device_id_type=MESH,
        )
    keep = pltpu.make_async_copy(piece_ref.at[z], held.at[z], own_sem)
    keep.start()
    pl.semaphore_wait(barrier, NZ - 1 + NY - 1)
    pieces = []
    half = CR // 2
    far = lax.rem(z + NZ // 2, NZ)
    first = pltpu.make_async_remote_copy(
        src_ref=piece_ref.at[far, pl.ds(half, half)],
        dst_ref=passing,
        send_sem=far_send.at[0],
        recv_sem=far_recv.at[0],
        device_id=device(x, lax.rem(z + NZ - 1, NZ), core, y),
        device_id_type=MESH,
    )
    first.start()
    direct = pltpu.make_async_remote_copy(
        src_ref=piece_ref.at[far, pl.ds(0, half)],
        dst_ref=held.at[z, pl.ds(0, half)],
        send_sem=far_send.at[1],
        recv_sem=far_recv.at[1],
        device_id=device(x, far, core, y),
        device_id_type=MESH,
    )
    direct.start()
    pieces.append(direct)
    for step in (3, 5, 2, 6, 1, 7):
        peer = lax.rem(z + step, NZ)
        copy = pltpu.make_async_remote_copy(
            src_ref=piece_ref.at[peer],
            dst_ref=held.at[z],
            send_sem=z_send.at[step],
            recv_sem=z_recv.at[step],
            device_id=device(x, peer, core, y),
            device_id_type=MESH,
        )
        copy.start()
        pieces.append(copy)

    def tap(k, t):
        return taps_ref[t]

    for part in range(0, B, 32):
        rowf[part : part + 32, :] = banded(
            (32, 256), lambda i, u: u - i - part - (STRIP - RADIUS), tap, 1
        )[0].astype(BF16)
    for part in range(0, 384, 64):
        colf[part : part + 64, :] = banded(
            (64, B), lambda m, l: m + part - B - l + RADIUS, tap, 1
        )[0].astype(BF16)
    padded[:, :B] = jnp.zeros((B, B), BF16)
    padded[:, B + CC * B :] = jnp.zeros((B, B), BF16)

    first.wait_recv()
    second = pltpu.make_async_remote_copy(
        src_ref=passing,
        dst_ref=held.at[lax.rem(z + 1, NZ), pl.ds(half, half)],
        send_sem=far_send.at[2],
        recv_sem=far_recv.at[2],
        device_id=device(x, lax.rem(z + 1 + NZ // 2, NZ), core, y),
        device_id_type=MESH,
    )
    second.start()
    pieces.append(second)
    keep.wait()
    first.wait_send()
    for copy in pieces:
        copy.wait()
    for r in range(CR):
        combined = held[0, r].astype(F32)
        for source in range(1, NZ):
            combined = combined + held[source, r].astype(F32)
        strips[r] = combined.astype(BF16)

    sends = []
    for step in range(1, NY):
        r = lax.rem(y + step, NY)
        copy = pltpu.make_async_remote_copy(
            src_ref=strips.at[r],
            dst_ref=window.at[1 + y],
            send_sem=y_send.at[step],
            recv_sem=y_recv.at[step],
            device_id=device(x, z, core, r),
            device_id_type=MESH,
        )
        copy.start()
        sends.append(copy)

    def edge(r, upper):
        return pltpu.make_async_remote_copy(
            src_ref=strips.at[r - 1 if upper else r + 1],
            dst_ref=window.at[0 if upper else NY + 1],
            send_sem=edge_send.at[r],
            recv_sem=edge_recv.at[0 if upper else 1],
            device_id=device(x, z, core, r),
            device_id_type=MESH,
        )

    @pl.when(y == NY - 1)
    def _():
        for r in range(1, NY - 1):
            edge(r, True).start()
        window[0] = strips[NY - 2]
        window[NY + 1] = jnp.zeros((STRIP, CC * B), BF16)

    @pl.when(y == 0)
    def _():
        for r in range(1, NY - 1):
            edge(r, False).start()
        window[0] = jnp.zeros((STRIP, CC * B), BF16)
        window[NY + 1] = strips[1]

    window[1 + y] = strips[y]
    for copy in sends:
        copy.wait()

    @pl.when((y > 0) & (y < NY - 1))
    def _():
        edge(1, True).wait_recv()
        edge(1, False).wait_recv()

    @pl.when(y == NY - 1)
    def _():
        for r in range(1, NY - 1):
            edge(r, True).wait_send()

    @pl.when(y == 0)
    def _():
        for r in range(1, NY - 1):
            edge(r, False).wait_send()

    for c in range(CC):
        at = slice(c * B, (c + 1) * B)
        padded[:, B + c * B : 2 * B + c * B] = jnp.dot(
            rowf[:, :ROWS], window[:, :, at].reshape(ROWS, B), preferred_element_type=F32
        ).astype(BF16)
    for c in range(CC):
        out_ref[:, c * B : (c + 1) * B] = jnp.dot(
            padded[:, c * B : c * B + 384], colf[...], preferred_element_type=F32
        )


def detect(taps, pieces):
    dma = pltpu.SemaphoreType.DMA
    return pl.pallas_call(
        detect_kernel,
        out_shape=jax.ShapeDtypeStruct((B, CC * B), F32),
        in_specs=[pl.BlockSpec(memory_space=pltpu.SMEM), pl.BlockSpec(memory_space=pl.ANY)],
        out_specs=pl.BlockSpec(memory_space=pltpu.VMEM),
        scratch_shapes=[
            pltpu.VMEM((NZ, CR, STRIP, CC * B), BF16),
            pltpu.VMEM((CR // 2, STRIP, CC * B), BF16),
            pltpu.VMEM((CR, STRIP, CC * B), BF16),
            pltpu.VMEM((NY + 2, STRIP, CC * B), BF16),
            pltpu.VMEM((B, 256), BF16),
            pltpu.VMEM((384, B), BF16),
            pltpu.VMEM((B, (CC + 2) * B), BF16),
            dma((NZ,)),
            dma((NZ,)),
            dma((3,)),
            dma((3,)),
            dma((NY,)),
            dma((NY,)),
            dma((NY,)),
            dma((2,)),
            dma,
        ],
        compiler_params=pltpu.CompilerParams(
            collective_id=1, has_side_effects=True, vmem_limit_bytes=8 * 1024 * 1024
        ),
        name="detect",
    )(taps, pieces)


def ranks(patch):
    earlier = jnp.arange(BLK)[None, :] < jnp.arange(BLK)[:, None]
    same = patch[..., :, None] == patch[..., None, :]
    return jnp.sum((same & earlier).astype(jnp.int32), axis=-1)


def local(
    raw_blocks,
    patch_of_block,
    cell_of_block,
    band_of_block,
    block_weight,
    basis_coef,
    row_basis,
    col_basis,
    band_gain,
    filter_taps,
):
    x, z, core, y = coordinates()
    patch = patch_of_block[:, 0]
    own_details = jnp.stack(
        [v.astype(F32) for v in (patch, cell_of_block, band_of_block, block_weight)]
    )
    patch_core = patch % NC
    patch_z = patch // NC % NZ
    patch_x = patch // (NC * NZ)
    slot = (patch_x * NC + patch_core) * (NY * SLOTS) + patch_z * CAP + ranks(patch)
    info, slot = lax.optimization_barrier((own_details.reshape(1, 1, 4 * BLK), slot))
    outgoing = match(slot, basis_coef.astype(F32), row_basis, col_basis, raw_blocks)
    arrived, details = plane_exchange(
        outgoing.reshape(PLANE, SLOTS, STRIP, B), info
    )
    details = details.reshape(NZ, PLANE, 4, BLK)

    my_patches = (x * NZ + jnp.arange(NZ, dtype=jnp.int32)) * NC + core
    every_patch = details[:, :, 0].astype(jnp.int32).reshape(-1)
    every_target = (details[:, :, 2] * CELLS + details[:, :, 1]).astype(jnp.int32).reshape(-1)
    every_weight = details[:, :, 3].reshape(-1)
    share = jnp.where(every_patch == my_patches[:, None], every_weight, 0.0).astype(BF16)
    hits = (every_target == jnp.arange(TARGETS, dtype=jnp.int32)[:, None]).astype(BF16)
    weight_sum = lax.dot_general(
        share, hits, (((1,), (1,)), ((), ())), preferred_element_type=F32
    )
    gain = (jnp.repeat(band_gain, CELLS) / jnp.maximum(weight_sum, 1.0)).reshape(-1)
    bins = (my_patches[:, None] * TARGETS + jnp.arange(TARGETS, dtype=jnp.int32)).reshape(-1)
    near = lax.dynamic_index_in_dim(details, z, axis=0, keepdims=False)
    near_names = near[:, :3].astype(jnp.int32)
    near_patch, near_cell = near_names[:, 0], near_names[:, 1]
    near_key = near_patch * TARGETS + near_names[:, 2] * CELLS + near_cell
    near_gain = jnp.sum(jnp.where(near_key[..., None] == bins, gain, 0.0), axis=-1)
    near_scale = near_gain * near[:, 3]
    near_rank = ranks(near_patch)
    chosen = (near_patch[:, None, None, :] == my_patches[:, None, None]) & (
        near_rank[:, None, None, :] == jnp.arange(CAP, dtype=jnp.int32)[:, None]
    )
    scale = jnp.sum(jnp.where(chosen, near_scale[:, None, None, :], 0.0), axis=-1).reshape(-1)
    cell = jnp.sum(jnp.where(chosen, near_cell[:, None, None, :] + 1, 0), axis=-1).reshape(-1) - 1

    pieces = gather_slots(cell, scale, arrived).reshape(NZ, CR, STRIP, CC * B)
    return detect(filter_taps, pieces)[None]


def solution(mesh):
    return jax.shard_map(
        local,
        mesh=mesh,
        in_specs=(
            P(None, ("sky", "band")),
            P(("sky", "band"), None),
            P(("sky", "band")),
            P(("sky", "band")),
            P(("sky", "band")),
            P(("sky", "band"), None),
            P(),
            P(),
            P(),
            P(),
        ),
        out_specs=P("sky", "band", None),
        check_vma=False,
    )
```

```python
import functools

import jax
import jax.numpy as jnp
from jax import lax
from jax.experimental import pallas as pl
from jax.experimental.pallas import tpu as pltpu
from jax.sharding import PartitionSpec as P

B = 128
TAPS = 41
RADIUS = 20
SIDE = 168
NBASIS = 3
BANDS = 6
CR = 4
CC = 4
CELLS = 16
TARGETS = BANDS * CELLS
BLK = 32
CAP = 2
NX, NZ, NC, NY = 4, 8, 2, 4
PLANE = NX * NC * NY
SLOTS = NZ * CAP
STRIP = B // NY
ROWS = B + 2 * STRIP
MESH = pl.DeviceIdType.MESH
HALFWAY = ((2, 2), (2, 0), (0, 2), (2, 1), (1, 2), (2, 3), (3, 2))
RELAYED = tuple((dx, 1, dy) for dx, dy in HALFWAY)
EARLY = tuple(
    (dx, dc, dy)
    for dx, dy in ((2, 2), (2, 0), (0, 2), (2, 1), (1, 2), (1, 1), (1, 0), (0, 1), (0, 0))
    for dc in range(NC)
    if (dx, dc, dy) != (0, 0, 0) and (dx, dc, dy) not in RELAYED
)
LATE = tuple(
    (dx, dc, dy)
    for dx, dy in ((2, 3), (3, 2), (3, 3), (1, 3), (3, 1), (3, 0), (0, 3))
    for dc in range(NC)
    if (dx, dc, dy) not in RELAYED
)
F32 = jnp.float32
BF16 = jnp.bfloat16


def coordinates():
    sky = lax.axis_index("sky")
    core = lax.rem(sky, NC)
    z = lax.rem(lax.div(sky, NC), NZ)
    x = lax.div(sky, NC * NZ)
    return x, z, core, lax.axis_index("band")


def device(x, z, core, y):
    return {"sky": (x * NZ + z) * NC + core, "band": y}


def banded(shape, diagonal, taps, rows):
    distance = diagonal(
        lax.broadcasted_iota(jnp.int32, shape, 0), lax.broadcasted_iota(jnp.int32, shape, 1)
    )

    def step(t, held):
        hit = distance == t
        return tuple(jnp.where(hit, taps(k, t), held[k]) for k in range(rows))

    return lax.fori_loop(0, TAPS, step, tuple(jnp.zeros(shape, F32) for _ in range(rows)))


def match_kernel(
    slot_ref, coef_ref, row_ref, col_ref, raw_ref, out_ref, rowk, colk, sectioned
):
    for part in range(0, B, 32):
        stack = banded((32, 256), lambda i, j: j - i - part, lambda k, t: row_ref[k, t], NBASIS)
        for k in range(NBASIS):
            rowk[k * B + part : k * B + part + 32, :] = stack[k].astype(BF16)
    colk[...] = jnp.zeros_like(colk)
    for part in range(0, 192, 64):
        for shift in range(2):
            stack = banded(
                (64, B),
                lambda u, l: u + part - l - 8 * shift,
                lambda k, t: col_ref[k, t],
                NBASIS,
            )
            for k in range(NBASIS):
                colk[shift, k, B + part : B + part + 64, :] = stack[k].astype(BF16)

    def clear(d, _):
        out_ref[pl.ds(d * SLOTS, SLOTS)] = jnp.zeros((SLOTS, STRIP, B), BF16)
        return 0

    lax.fori_loop(0, PLANE, clear, 0)

    def rows(step, _):
        at = pl.ds(pl.multiple_of(step * 256, 256), 256)
        sectioned[:, at] = jnp.dot(
            rowk[:, :SIDE], raw_ref[:, at], preferred_element_type=F32
        ).astype(BF16)
        return 0

    lax.fori_loop(0, BLK * SIDE // 256, rows, 0)

    def columns(group, _):
        for j in range(16):
            first = j * SIDE // B * B
            offset = j * SIDE - first
            width = 256 if offset + SIDE <= 256 else 384
            shift = offset // 8 % 2
            start = B - offset + 8 * shift
            at = pl.ds(pl.multiple_of(group * (16 * SIDE) + first, B), width)
            block = group * 16 + j
            total = None
            for k in range(NBASIS):
                term = coef_ref[block, k] * jnp.dot(
                    sectioned[k * B : (k + 1) * B, at],
                    colk[shift, k, start : start + width, :],
                    preferred_element_type=F32,
                )
                total = term if total is None else total + term
            slot = slot_ref[block]
            for strip in range(NY):
                out_ref[slot + strip * SLOTS] = total[strip * STRIP : (strip + 1) * STRIP].astype(
                    BF16
                )
        return 0

    lax.fori_loop(0, BLK // 16, columns, 0)


def match(slot, coef, row_basis, col_basis, raw):
    smem = pl.BlockSpec(memory_space=pltpu.SMEM)
    vmem = pl.BlockSpec(memory_space=pltpu.VMEM)
    return pl.pallas_call(
        match_kernel,
        out_shape=jax.ShapeDtypeStruct((PLANE * SLOTS, STRIP, B), BF16),
        in_specs=[smem, smem, smem, smem, vmem],
        out_specs=vmem,
        scratch_shapes=[
            pltpu.VMEM((NBASIS * B, 256), BF16),
            pltpu.VMEM((2, NBASIS, 512, B), BF16),
            pltpu.VMEM((NBASIS * B, BLK * SIDE), BF16),
        ],
        compiler_params=pltpu.CompilerParams(vmem_limit_bytes=24 * 1024 * 1024),
        name="match",
    )(slot, coef, row_basis, col_basis, raw)


def offset_id(offset):
    dx, dc, dy = offset
    return (dx * NC + dc) * NY + dy


def plane_kernel(
    out_ref,
    info_ref,
    in_ref,
    every_ref,
    own,
    passing,
    send_sem,
    recv_sem,
    pass_send,
    pass_recv,
    info_send,
    info_recv,
    z_send,
    z_recv,
    own_sem,
    info_sem,
):
    x, z, core, y = coordinates()
    me = (x * NC + core) * NY + y

    def moved(dx, dc, dy):
        return lax.rem(x + dx, NX), lax.rem(core + dc, NC), lax.rem(y + dy, NY)

    def index(place):
        return (place[0] * NC + place[1]) * NY + place[2]

    def at(place):
        return device(place[0], z, place[1], place[2])

    everyone = RELAYED + EARLY + LATE
    barrier = pltpu.get_barrier_semaphore()
    for offset in everyone:
        pl.semaphore_signal(barrier, inc=1, device_id=at(moved(*offset)), device_id_type=MESH)
    for step in range(1, NZ):
        pl.semaphore_signal(
            barrier,
            inc=1,
            device_id=device(x, lax.rem(z + step, NZ), core, y),
            device_id_type=MESH,
        )
    take = pltpu.make_async_copy(out_ref.at[me], own, own_sem)
    take.start()
    keep = pltpu.make_async_copy(info_ref.at[0], every_ref.at[z, me], info_sem)
    keep.start()
    pl.semaphore_wait(barrier, PLANE - 1 + NZ - 1)
    infos = []
    for offset in everyone:
        copy = pltpu.make_async_remote_copy(
            src_ref=info_ref.at[0],
            dst_ref=every_ref.at[z, me],
            send_sem=info_send.at[offset_id(offset)],
            recv_sem=info_recv.at[offset_id(offset)],
            device_id=at(moved(*offset)),
            device_id_type=MESH,
        )
        copy.start()
        infos.append(copy)
    firsts = []
    for k, (dx, dc, dy) in enumerate(RELAYED):
        back_x, back_y = (NX - 1) * (dx == 2), (NY - 1) * (dy == 2)
        copy = pltpu.make_async_remote_copy(
            src_ref=out_ref.at[index(moved(dx, dc, dy))],
            dst_ref=passing.at[k],
            send_sem=pass_send.at[k],
            recv_sem=pass_recv.at[k],
            device_id=at(moved(back_x, 0, back_y)),
            device_id_type=MESH,
        )
        copy.start()
        firsts.append(copy)
    copies = []

    def send(offset):
        copy = pltpu.make_async_remote_copy(
            src_ref=out_ref.at[index(moved(*offset))],
            dst_ref=in_ref.at[me],
            send_sem=send_sem.at[offset_id(offset)],
            recv_sem=recv_sem.at[offset_id(offset)],
            device_id=at(moved(*offset)),
            device_id_type=MESH,
        )
        copy.start()
        copies.append(copy)

    for offset in EARLY:
        send(offset)
    take.wait()
    put = pltpu.make_async_copy(own, in_ref.at[me], own_sem)
    put.start()
    for k, offset in enumerate(RELAYED):
        dx, dc, dy = offset
        ahead_x, ahead_y = dx == 2, dy == 2
        firsts[k].wait_recv()
        copy = pltpu.make_async_remote_copy(
            src_ref=passing.at[k],
            dst_ref=in_ref.at[index(moved(int(ahead_x), 0, int(ahead_y)))],
            send_sem=send_sem.at[offset_id(offset)],
            recv_sem=recv_sem.at[offset_id(offset)],
            device_id=at(moved((dx + ahead_x) % NX, dc, (dy + ahead_y) % NY)),
            device_id_type=MESH,
        )
        copy.start()
        copies.append(copy)
    for offset in LATE:
        send(offset)
    keep.wait()
    for copy in infos:
        copy.wait()
    planes = []
    for step in range(1, NZ):
        copy = pltpu.make_async_remote_copy(
            src_ref=every_ref.at[z],
            dst_ref=every_ref.at[z],
            send_sem=z_send.at[step],
            recv_sem=z_recv.at[step],
            device_id=device(x, lax.rem(z + step, NZ), core, y),
            device_id_type=MESH,
        )
        copy.start()
        planes.append(copy)
    put.wait()
    for copy in planes:
        copy.wait()
    for copy in firsts:
        copy.wait_send()
    for copy in copies:
        copy.wait()


def plane_exchange(outgoing, info):
    hbm = pl.BlockSpec(memory_space=pl.ANY)
    vmem = pl.BlockSpec(memory_space=pltpu.VMEM)
    dma = pltpu.SemaphoreType.DMA
    return pl.pallas_call(
        plane_kernel,
        out_shape=(
            jax.ShapeDtypeStruct((PLANE, SLOTS, STRIP, B), BF16),
            jax.ShapeDtypeStruct((NZ, PLANE, 1, B), F32),
        ),
        in_specs=[hbm, vmem],
        out_specs=(pl.BlockSpec(memory_space=pltpu.HBM), vmem),
        scratch_shapes=[
            pltpu.VMEM((SLOTS, STRIP, B), BF16),
            pltpu.VMEM((len(RELAYED), SLOTS, STRIP, B), BF16),
            dma((PLANE,)),
            dma((PLANE,)),
            dma((len(RELAYED),)),
            dma((len(RELAYED),)),
            dma((PLANE,)),
            dma((PLANE,)),
            dma((NZ,)),
            dma((NZ,)),
            dma,
            dma,
        ],
        compiler_params=pltpu.CompilerParams(
            collective_id=0, has_side_effects=True, vmem_limit_bytes=4 * 1024 * 1024
        ),
        name="plane_exchange",
    )(outgoing, info)


def gather_kernel(cell_ref, scale_ref, in_ref, out_ref, total):
    step = pl.program_id(0)
    per_step = in_ref.shape[0]

    @pl.when(step == 0)
    def _():
        def clear(i, _):
            total[i] = jnp.zeros((STRIP, CC * B), F32)
            return 0

        lax.fori_loop(0, NZ * CR, clear, 0)

    for d in range(per_step):
        for s in range(SLOTS):
            slot = (step * per_step + d) * SLOTS + s
            cell = cell_ref[slot]

            @pl.when(cell >= 0)
            def _():
                row = (s // CAP) * CR + lax.div(cell, CC)
                column = pl.multiple_of(lax.rem(cell, CC) * B, B)
                total[row, :, pl.ds(column, B)] += scale_ref[slot] * in_ref[d, s].astype(F32)

    @pl.when(step == pl.num_programs(0) - 1)
    def _():
        def write(i, _):
            out_ref[i] = total[i].astype(BF16)
            return 0

        lax.fori_loop(0, NZ * CR, write, 0)


def gather_slots(cell, scale, arrived):
    smem = pl.BlockSpec(memory_space=pltpu.SMEM)
    per_step = 4
    shape = (NZ * CR, STRIP, CC * B)
    return pl.pallas_call(
        gather_kernel,
        grid=(PLANE // per_step,),
        out_shape=jax.ShapeDtypeStruct(shape, BF16),
        in_specs=[smem, smem, pl.BlockSpec((per_step, SLOTS, STRIP, B), lambda i: (i, 0, 0, 0))],
        out_specs=pl.BlockSpec(shape, lambda i: (0, 0, 0)),
        scratch_shapes=[pltpu.VMEM(shape, F32)],
        compiler_params=pltpu.CompilerParams(vmem_limit_bytes=60 * 1024 * 1024),
        name="gather_slots",
    )(cell, scale, arrived)


def detect_kernel(
    taps_ref,
    piece_ref,
    out_ref,
    held,
    passing,
    strips,
    window,
    rowf,
    colf,
    padded,
    z_send,
    z_recv,
    far_send,
    far_recv,
    y_send,
    y_recv,
    edge_send,
    edge_recv,
    own_sem,
):
    x, z, core, y = coordinates()
    barrier = pltpu.get_barrier_semaphore()
    for step in range(1, NZ):
        pl.semaphore_signal(
            barrier,
            inc=1,
            device_id=device(x, lax.rem(z + step, NZ), core, y),
            device_id_type=MESH,
        )
    for step in range(1, NY):
        pl.semaphore_signal(
            barrier,
            inc=1,
            device_id=device(x, z, core, lax.rem(y + step, NY)),
            device_id_type=MESH,
        )
    keep = pltpu.make_async_copy(piece_ref.at[z], held.at[z], own_sem)
    keep.start()
    pl.semaphore_wait(barrier, NZ - 1 + NY - 1)
    pieces = []
    half = CR // 2
    far = lax.rem(z + NZ // 2, NZ)
    first = pltpu.make_async_remote_copy(
        src_ref=piece_ref.at[far, pl.ds(half, half)],
        dst_ref=passing,
        send_sem=far_send.at[0],
        recv_sem=far_recv.at[0],
        device_id=device(x, lax.rem(z + NZ - 1, NZ), core, y),
        device_id_type=MESH,
    )
    first.start()
    direct = pltpu.make_async_remote_copy(
        src_ref=piece_ref.at[far, pl.ds(0, half)],
        dst_ref=held.at[z, pl.ds(0, half)],
        send_sem=far_send.at[1],
        recv_sem=far_recv.at[1],
        device_id=device(x, far, core, y),
        device_id_type=MESH,
    )
    direct.start()
    pieces.append(direct)

    def send(step):
        peer = lax.rem(z + step, NZ)
        copy = pltpu.make_async_remote_copy(
            src_ref=piece_ref.at[peer],
            dst_ref=held.at[z],
            send_sem=z_send.at[step],
            recv_sem=z_recv.at[step],
            device_id=device(x, peer, core, y),
            device_id_type=MESH,
        )
        copy.start()
        pieces.append(copy)

    for step in (3, 2, 1, 7):
        send(step)
    first.wait_recv()
    second = pltpu.make_async_remote_copy(
        src_ref=passing,
        dst_ref=held.at[lax.rem(z + 1, NZ), pl.ds(half, half)],
        send_sem=far_send.at[2],
        recv_sem=far_recv.at[2],
        device_id=device(x, lax.rem(z + 1 + NZ // 2, NZ), core, y),
        device_id_type=MESH,
    )
    second.start()
    pieces.append(second)
    for step in (5, 6):
        send(step)

    def tap(k, t):
        return taps_ref[t]

    for part in range(0, B, 32):
        rowf[part : part + 32, :] = banded(
            (32, 256), lambda i, u: u - i - part - (STRIP - RADIUS), tap, 1
        )[0].astype(BF16)
    for part in range(0, 384, 64):
        colf[part : part + 64, :] = banded(
            (64, B), lambda m, l: m + part - B - l + RADIUS, tap, 1
        )[0].astype(BF16)
    padded[:, :B] = jnp.zeros((B, B), BF16)
    padded[:, B + CC * B :] = jnp.zeros((B, B), BF16)

    keep.wait()
    first.wait_send()
    for copy in pieces:
        copy.wait()
    for r in range(CR):
        combined = held[0, r].astype(F32)
        for source in range(1, NZ):
            combined = combined + held[source, r].astype(F32)
        strips[r] = combined.astype(BF16)

    sends = []
    for step in range(1, NY):
        r = lax.rem(y + step, NY)
        copy = pltpu.make_async_remote_copy(
            src_ref=strips.at[r],
            dst_ref=window.at[1 + y],
            send_sem=y_send.at[step],
            recv_sem=y_recv.at[step],
            device_id=device(x, z, core, r),
            device_id_type=MESH,
        )
        copy.start()
        sends.append(copy)

    def edge(r, upper):
        return pltpu.make_async_remote_copy(
            src_ref=strips.at[r - 1 if upper else r + 1],
            dst_ref=window.at[0 if upper else NY + 1],
            send_sem=edge_send.at[r],
            recv_sem=edge_recv.at[0 if upper else 1],
            device_id=device(x, z, core, r),
            device_id_type=MESH,
        )

    @pl.when(y == NY - 1)
    def _():
        for r in range(1, NY - 1):
            edge(r, True).start()
        window[0] = strips[NY - 2]
        window[NY + 1] = jnp.zeros((STRIP, CC * B), BF16)

    @pl.when(y == 0)
    def _():
        for r in range(1, NY - 1):
            edge(r, False).start()
        window[0] = jnp.zeros((STRIP, CC * B), BF16)
        window[NY + 1] = strips[1]

    window[1 + y] = strips[y]
    for copy in sends:
        copy.wait()

    @pl.when((y > 0) & (y < NY - 1))
    def _():
        edge(1, True).wait_recv()
        edge(1, False).wait_recv()

    @pl.when(y == NY - 1)
    def _():
        for r in range(1, NY - 1):
            edge(r, True).wait_send()

    @pl.when(y == 0)
    def _():
        for r in range(1, NY - 1):
            edge(r, False).wait_send()

    for c in range(CC):
        at = slice(c * B, (c + 1) * B)
        padded[:, B + c * B : 2 * B + c * B] = jnp.dot(
            rowf[:, :ROWS], window[:, :, at].reshape(ROWS, B), preferred_element_type=F32
        ).astype(BF16)
    for c in range(CC):
        out_ref[:, c * B : (c + 1) * B] = jnp.dot(
            padded[:, c * B : c * B + 384], colf[...], preferred_element_type=F32
        )


def detect(taps, pieces):
    dma = pltpu.SemaphoreType.DMA
    return pl.pallas_call(
        detect_kernel,
        out_shape=jax.ShapeDtypeStruct((B, CC * B), F32),
        in_specs=[pl.BlockSpec(memory_space=pltpu.SMEM), pl.BlockSpec(memory_space=pl.ANY)],
        out_specs=pl.BlockSpec(memory_space=pltpu.VMEM),
        scratch_shapes=[
            pltpu.VMEM((NZ, CR, STRIP, CC * B), BF16),
            pltpu.VMEM((CR // 2, STRIP, CC * B), BF16),
            pltpu.VMEM((CR, STRIP, CC * B), BF16),
            pltpu.VMEM((NY + 2, STRIP, CC * B), BF16),
            pltpu.VMEM((B, 256), BF16),
            pltpu.VMEM((384, B), BF16),
            pltpu.VMEM((B, (CC + 2) * B), BF16),
            dma((NZ,)),
            dma((NZ,)),
            dma((3,)),
            dma((3,)),
            dma((NY,)),
            dma((NY,)),
            dma((NY,)),
            dma((2,)),
            dma,
        ],
        compiler_params=pltpu.CompilerParams(
            collective_id=1, has_side_effects=True, vmem_limit_bytes=8 * 1024 * 1024
        ),
        name="detect",
    )(taps, pieces)


def ranks(patch):
    earlier = jnp.arange(BLK)[None, :] < jnp.arange(BLK)[:, None]
    same = patch[..., :, None] == patch[..., None, :]
    return jnp.sum((same & earlier).astype(jnp.int32), axis=-1)


def local(
    raw_blocks,
    patch_of_block,
    cell_of_block,
    band_of_block,
    block_weight,
    basis_coef,
    row_basis,
    col_basis,
    band_gain,
    filter_taps,
):
    x, z, core, y = coordinates()
    patch = patch_of_block[:, 0]
    rank = ranks(patch)
    target = band_of_block * CELLS + cell_of_block
    own_details = jnp.stack([v.astype(F32) for v in (patch, target, rank, block_weight)])
    patch_core = patch % NC
    patch_z = patch // NC % NZ
    patch_x = patch // (NC * NZ)
    slot = (patch_x * NC + patch_core) * (NY * SLOTS) + patch_z * CAP + rank
    info, slot = lax.optimization_barrier((own_details.reshape(1, 1, 4 * BLK), slot))
    outgoing = match(slot, basis_coef.astype(F32), row_basis, col_basis, raw_blocks)
    arrived, details = plane_exchange(
        outgoing.reshape(PLANE, SLOTS, STRIP, B), info
    )
    details = details.reshape(NZ, PLANE, 4, BLK)

    my_patches = (x * NZ + jnp.arange(NZ, dtype=jnp.int32)) * NC + core
    every_patch = details[:, :, 0].astype(jnp.int32).reshape(-1)
    every_target = details[:, :, 1].astype(jnp.int32).reshape(-1)
    every_weight = details[:, :, 3].reshape(-1)
    share = jnp.where(every_patch == my_patches[:, None], every_weight, 0.0).astype(BF16)
    hits = (every_target == jnp.arange(TARGETS, dtype=jnp.int32)[:, None]).astype(BF16)
    weight_sum = lax.dot_general(
        share, hits, (((1,), (1,)), ((), ())), preferred_element_type=F32
    )
    gain = (jnp.repeat(band_gain, CELLS) / jnp.maximum(weight_sum, 1.0)).reshape(-1)
    bins = (my_patches[:, None] * TARGETS + jnp.arange(TARGETS, dtype=jnp.int32)).reshape(-1)
    near = lax.dynamic_index_in_dim(details, z, axis=0, keepdims=False)
    near_names = near[:, :3].astype(jnp.int32)
    near_patch, near_target, near_rank = near_names[:, 0], near_names[:, 1], near_names[:, 2]
    near_cell = near_target % CELLS
    near_key = near_patch * TARGETS + near_target
    near_gain = jnp.sum(jnp.where(near_key[..., None] == bins, gain, 0.0), axis=-1)
    near_scale = near_gain * near[:, 3]
    chosen = (near_patch[:, None, None, :] == my_patches[:, None, None]) & (
        near_rank[:, None, None, :] == jnp.arange(CAP, dtype=jnp.int32)[:, None]
    )
    scale = jnp.sum(jnp.where(chosen, near_scale[:, None, None, :], 0.0), axis=-1).reshape(-1)
    cell = jnp.sum(jnp.where(chosen, near_cell[:, None, None, :] + 1, 0), axis=-1).reshape(-1) - 1

    pieces = gather_slots(cell, scale, arrived).reshape(NZ, CR, STRIP, CC * B)
    return detect(filter_taps, pieces)[None]


def solution(mesh):
    return jax.shard_map(
        local,
        mesh=mesh,
        in_specs=(
            P(None, ("sky", "band")),
            P(("sky", "band"), None),
            P(("sky", "band")),
            P(("sky", "band")),
            P(("sky", "band")),
            P(("sky", "band"), None),
            P(),
            P(),
            P(),
            P(),
        ),
        out_specs=P("sky", "band", None),
        check_vma=False,
    )
```

```python
import functools

import jax
import jax.numpy as jnp
from jax import lax
from jax.experimental import pallas as pl
from jax.experimental.pallas import tpu as pltpu
from jax.sharding import PartitionSpec as P

B = 128
TAPS = 41
RADIUS = 20
SIDE = 168
NBASIS = 3
BANDS = 6
CR = 4
CC = 4
CELLS = 16
TARGETS = BANDS * CELLS
BLK = 32
CAP = 2
NX, NZ, NC, NY = 4, 8, 2, 4
PLANE = NX * NC * NY
SLOTS = NZ * CAP
STRIP = B // NY
ROWS = B + 2 * STRIP
MESH = pl.DeviceIdType.MESH
HALFWAY = ((2, 2), (2, 0), (0, 2), (2, 1), (1, 2), (2, 3), (3, 2))
RELAYED = tuple((dx, 1, dy) for dx, dy in HALFWAY)
DIRECT = tuple((dx, 0, dy) for dx, dy in HALFWAY) + tuple(
    (dx, dc, dy)
    for dx, dy in ((1, 3), (3, 1), (1, 1), (3, 3), (1, 0), (3, 0), (0, 1), (0, 3), (0, 0))
    for dc in range(NC)
    if (dx, dc, dy) != (0, 0, 0)
)
F32 = jnp.float32
BF16 = jnp.bfloat16


def coordinates():
    sky = lax.axis_index("sky")
    core = lax.rem(sky, NC)
    z = lax.rem(lax.div(sky, NC), NZ)
    x = lax.div(sky, NC * NZ)
    return x, z, core, lax.axis_index("band")


def device(x, z, core, y):
    return {"sky": (x * NZ + z) * NC + core, "band": y}


def banded(shape, diagonal, taps, rows):
    distance = diagonal(
        lax.broadcasted_iota(jnp.int32, shape, 0), lax.broadcasted_iota(jnp.int32, shape, 1)
    )

    def step(t, held):
        hit = distance == t
        return tuple(jnp.where(hit, taps(k, t), held[k]) for k in range(rows))

    return lax.fori_loop(0, TAPS, step, tuple(jnp.zeros(shape, F32) for _ in range(rows)))


def match_kernel(
    slot_ref, coef_ref, row_ref, col_ref, raw_ref, out_ref, rowk, colk, sectioned
):
    for part in range(0, B, 32):
        stack = banded((32, 256), lambda i, j: j - i - part, lambda k, t: row_ref[k, t], NBASIS)
        for k in range(NBASIS):
            rowk[k * B + part : k * B + part + 32, :] = stack[k].astype(BF16)
    colk[...] = jnp.zeros_like(colk)
    for part in range(0, 192, 64):
        for shift in range(2):
            stack = banded(
                (64, B),
                lambda u, l: u + part - l - 8 * shift,
                lambda k, t: col_ref[k, t],
                NBASIS,
            )
            for k in range(NBASIS):
                colk[shift, k, B + part : B + part + 64, :] = stack[k].astype(BF16)

    def clear(d, _):
        out_ref[pl.ds(d * SLOTS, SLOTS)] = jnp.zeros((SLOTS, STRIP, B), BF16)
        return 0

    lax.fori_loop(0, PLANE, clear, 0)

    def rows(step, _):
        at = pl.ds(pl.multiple_of(step * 256, 256), 256)
        sectioned[:, at] = jnp.dot(
            rowk[:, :SIDE], raw_ref[:, at], preferred_element_type=F32
        ).astype(BF16)
        return 0

    lax.fori_loop(0, BLK * SIDE // 256, rows, 0)

    def columns(group, _):
        for j in range(16):
            first = j * SIDE // B * B
            offset = j * SIDE - first
            width = 256 if offset + SIDE <= 256 else 384
            shift = offset // 8 % 2
            start = B - offset + 8 * shift
            at = pl.ds(pl.multiple_of(group * (16 * SIDE) + first, B), width)
            block = group * 16 + j
            total = None
            for k in range(NBASIS):
                term = coef_ref[block, k] * jnp.dot(
                    sectioned[k * B : (k + 1) * B, at],
                    colk[shift, k, start : start + width, :],
                    preferred_element_type=F32,
                )
                total = term if total is None else total + term
            slot = slot_ref[block]
            for strip in range(NY):
                out_ref[slot + strip * SLOTS] = total[strip * STRIP : (strip + 1) * STRIP].astype(
                    BF16
                )
        return 0

    lax.fori_loop(0, BLK // 16, columns, 0)


def match(slot, coef, row_basis, col_basis, raw):
    smem = pl.BlockSpec(memory_space=pltpu.SMEM)
    vmem = pl.BlockSpec(memory_space=pltpu.VMEM)
    return pl.pallas_call(
        match_kernel,
        out_shape=jax.ShapeDtypeStruct((PLANE * SLOTS, STRIP, B), BF16),
        in_specs=[smem, smem, smem, smem, vmem],
        out_specs=vmem,
        scratch_shapes=[
            pltpu.VMEM((NBASIS * B, 256), BF16),
            pltpu.VMEM((2, NBASIS, 512, B), BF16),
            pltpu.VMEM((NBASIS * B, BLK * SIDE), BF16),
        ],
        compiler_params=pltpu.CompilerParams(vmem_limit_bytes=24 * 1024 * 1024),
        name="match",
    )(slot, coef, row_basis, col_basis, raw)


def offset_id(offset):
    dx, dc, dy = offset
    return (dx * NC + dc) * NY + dy


def plane_kernel(
    out_ref,
    info_ref,
    in_ref,
    every_ref,
    own,
    passing,
    send_sem,
    recv_sem,
    pass_send,
    pass_recv,
    info_send,
    info_recv,
    z_send,
    z_recv,
    own_sem,
    info_sem,
):
    x, z, core, y = coordinates()
    me = (x * NC + core) * NY + y

    def moved(dx, dc, dy):
        return lax.rem(x + dx, NX), lax.rem(core + dc, NC), lax.rem(y + dy, NY)

    def index(place):
        return (place[0] * NC + place[1]) * NY + place[2]

    def at(place):
        return device(place[0], z, place[1], place[2])

    everyone = RELAYED + DIRECT
    barrier = pltpu.get_barrier_semaphore()
    for offset in everyone:
        pl.semaphore_signal(barrier, inc=1, device_id=at(moved(*offset)), device_id_type=MESH)
    for step in range(1, NZ):
        pl.semaphore_signal(
            barrier,
            inc=1,
            device_id=device(x, lax.rem(z + step, NZ), core, y),
            device_id_type=MESH,
        )
    take = pltpu.make_async_copy(out_ref.at[me], own, own_sem)
    take.start()
    keep = pltpu.make_async_copy(info_ref.at[0], every_ref.at[z, me], info_sem)
    keep.start()
    pl.semaphore_wait(barrier, PLANE - 1 + NZ - 1)
    infos = []
    for offset in everyone:
        copy = pltpu.make_async_remote_copy(
            src_ref=info_ref.at[0],
            dst_ref=every_ref.at[z, me],
            send_sem=info_send.at[offset_id(offset)],
            recv_sem=info_recv.at[offset_id(offset)],
            device_id=at(moved(*offset)),
            device_id_type=MESH,
        )
        copy.start()
        infos.append(copy)
    firsts = []
    for k, (dx, dc, dy) in enumerate(RELAYED):
        back_x, back_y = (NX - 1) * (dx == 2), (NY - 1) * (dy == 2)
        copy = pltpu.make_async_remote_copy(
            src_ref=out_ref.at[index(moved(dx, dc, dy))],
            dst_ref=passing.at[k],
            send_sem=pass_send.at[k],
            recv_sem=pass_recv.at[k],
            device_id=at(moved(back_x, 0, back_y)),
            device_id_type=MESH,
        )
        copy.start()
        firsts.append(copy)
    copies = []

    def send(offset):
        copy = pltpu.make_async_remote_copy(
            src_ref=out_ref.at[index(moved(*offset))],
            dst_ref=in_ref.at[me],
            send_sem=send_sem.at[offset_id(offset)],
            recv_sem=recv_sem.at[offset_id(offset)],
            device_id=at(moved(*offset)),
            device_id_type=MESH,
        )
        copy.start()
        copies.append(copy)

    for offset in DIRECT:
        send(offset)
    take.wait()
    put = pltpu.make_async_copy(own, in_ref.at[me], own_sem)
    put.start()
    for k, offset in enumerate(RELAYED):
        dx, dc, dy = offset
        ahead_x, ahead_y = dx == 2, dy == 2
        firsts[k].wait_recv()
        copy = pltpu.make_async_remote_copy(
            src_ref=passing.at[k],
            dst_ref=in_ref.at[index(moved(int(ahead_x), 0, int(ahead_y)))],
            send_sem=send_sem.at[offset_id(offset)],
            recv_sem=recv_sem.at[offset_id(offset)],
            device_id=at(moved((dx + ahead_x) % NX, dc, (dy + ahead_y) % NY)),
            device_id_type=MESH,
        )
        copy.start()
        copies.append(copy)
    keep.wait()
    for copy in infos:
        copy.wait()
    planes = []
    for step in range(1, NZ):
        copy = pltpu.make_async_remote_copy(
            src_ref=every_ref.at[z],
            dst_ref=every_ref.at[z],
            send_sem=z_send.at[step],
            recv_sem=z_recv.at[step],
            device_id=device(x, lax.rem(z + step, NZ), core, y),
            device_id_type=MESH,
        )
        copy.start()
        planes.append(copy)
    put.wait()
    for copy in planes:
        copy.wait()
    for copy in firsts:
        copy.wait_send()
    for copy in copies:
        copy.wait()


def plane_exchange(outgoing, info):
    hbm = pl.BlockSpec(memory_space=pl.ANY)
    vmem = pl.BlockSpec(memory_space=pltpu.VMEM)
    dma = pltpu.SemaphoreType.DMA
    return pl.pallas_call(
        plane_kernel,
        out_shape=(
            jax.ShapeDtypeStruct((PLANE, SLOTS, STRIP, B), BF16),
            jax.ShapeDtypeStruct((NZ, PLANE, 1, B), F32),
        ),
        in_specs=[hbm, vmem],
        out_specs=(pl.BlockSpec(memory_space=pltpu.HBM), vmem),
        scratch_shapes=[
            pltpu.VMEM((SLOTS, STRIP, B), BF16),
            pltpu.VMEM((len(RELAYED), SLOTS, STRIP, B), BF16),
            dma((PLANE,)),
            dma((PLANE,)),
            dma((len(RELAYED),)),
            dma((len(RELAYED),)),
            dma((PLANE,)),
            dma((PLANE,)),
            dma((NZ,)),
            dma((NZ,)),
            dma,
            dma,
        ],
        compiler_params=pltpu.CompilerParams(
            collective_id=0, has_side_effects=True, vmem_limit_bytes=4 * 1024 * 1024
        ),
        name="plane_exchange",
    )(outgoing, info)


def gather_kernel(cell_ref, scale_ref, in_ref, out_ref, total):
    step = pl.program_id(0)
    per_step = in_ref.shape[0]

    @pl.when(step == 0)
    def _():
        def clear(i, _):
            total[i] = jnp.zeros((STRIP, CC * B), F32)
            return 0

        lax.fori_loop(0, NZ * CR, clear, 0)

    for d in range(per_step):
        for s in range(SLOTS):
            slot = (step * per_step + d) * SLOTS + s
            cell = cell_ref[slot]

            @pl.when(cell >= 0)
            def _():
                row = (s // CAP) * CR + lax.div(cell, CC)
                column = pl.multiple_of(lax.rem(cell, CC) * B, B)
                total[row, :, pl.ds(column, B)] += scale_ref[slot] * in_ref[d, s].astype(F32)

    @pl.when(step == pl.num_programs(0) - 1)
    def _():
        def write(i, _):
            out_ref[i] = total[i].astype(BF16)
            return 0

        lax.fori_loop(0, NZ * CR, write, 0)


def gather_slots(cell, scale, arrived):
    smem = pl.BlockSpec(memory_space=pltpu.SMEM)
    per_step = 4
    shape = (NZ * CR, STRIP, CC * B)
    return pl.pallas_call(
        gather_kernel,
        grid=(PLANE // per_step,),
        out_shape=jax.ShapeDtypeStruct(shape, BF16),
        in_specs=[smem, smem, pl.BlockSpec((per_step, SLOTS, STRIP, B), lambda i: (i, 0, 0, 0))],
        out_specs=pl.BlockSpec(shape, lambda i: (0, 0, 0)),
        scratch_shapes=[pltpu.VMEM(shape, F32)],
        compiler_params=pltpu.CompilerParams(vmem_limit_bytes=16 * 1024 * 1024),
        name="gather_slots",
    )(cell, scale, arrived)


def detect_kernel(
    taps_ref,
    piece_ref,
    out_ref,
    held,
    passing,
    strips,
    window,
    rowf,
    colf,
    padded,
    z_send,
    z_recv,
    far_send,
    far_recv,
    y_send,
    y_recv,
    edge_send,
    edge_recv,
    own_sem,
):
    x, z, core, y = coordinates()
    barrier = pltpu.get_barrier_semaphore()
    for step in range(1, NZ):
        pl.semaphore_signal(
            barrier,
            inc=1,
            device_id=device(x, lax.rem(z + step, NZ), core, y),
            device_id_type=MESH,
        )
    for step in range(1, NY):
        pl.semaphore_signal(
            barrier,
            inc=1,
            device_id=device(x, z, core, lax.rem(y + step, NY)),
            device_id_type=MESH,
        )
    keep = pltpu.make_async_copy(piece_ref.at[z], held.at[z], own_sem)
    keep.start()
    pl.semaphore_wait(barrier, NZ - 1 + NY - 1)
    pieces = []
    half = CR // 2
    far = lax.rem(z + NZ // 2, NZ)
    first = pltpu.make_async_remote_copy(
        src_ref=piece_ref.at[far, pl.ds(half, half)],
        dst_ref=passing,
        send_sem=far_send.at[0],
        recv_sem=far_recv.at[0],
        device_id=device(x, lax.rem(z + NZ - 1, NZ), core, y),
        device_id_type=MESH,
    )
    first.start()
    direct = pltpu.make_async_remote_copy(
        src_ref=piece_ref.at[far, pl.ds(0, half)],
        dst_ref=held.at[z, pl.ds(0, half)],
        send_sem=far_send.at[1],
        recv_sem=far_recv.at[1],
        device_id=device(x, far, core, y),
        device_id_type=MESH,
    )
    direct.start()
    pieces.append(direct)

    def send(step):
        peer = lax.rem(z + step, NZ)
        copy = pltpu.make_async_remote_copy(
            src_ref=piece_ref.at[peer],
            dst_ref=held.at[z],
            send_sem=z_send.at[step],
            recv_sem=z_recv.at[step],
            device_id=device(x, peer, core, y),
            device_id_type=MESH,
        )
        copy.start()
        pieces.append(copy)

    for step in (3, 2, 1, 7):
        send(step)
    first.wait_recv()
    second = pltpu.make_async_remote_copy(
        src_ref=passing,
        dst_ref=held.at[lax.rem(z + 1, NZ), pl.ds(half, half)],
        send_sem=far_send.at[2],
        recv_sem=far_recv.at[2],
        device_id=device(x, lax.rem(z + 1 + NZ // 2, NZ), core, y),
        device_id_type=MESH,
    )
    second.start()
    pieces.append(second)
    for step in (5, 6):
        send(step)

    def tap(k, t):
        return taps_ref[t]

    for part in range(0, B, 32):
        rowf[part : part + 32, :] = banded(
            (32, 256), lambda i, u: u - i - part - (STRIP - RADIUS), tap, 1
        )[0].astype(BF16)
    for part in range(0, 384, 64):
        colf[part : part + 64, :] = banded(
            (64, B), lambda m, l: m + part - B - l + RADIUS, tap, 1
        )[0].astype(BF16)
    padded[:, :B] = jnp.zeros((B, B), BF16)
    padded[:, B + CC * B :] = jnp.zeros((B, B), BF16)

    keep.wait()
    first.wait_send()
    for copy in pieces:
        copy.wait()
    for r in range(CR):
        combined = held[0, r].astype(F32)
        for source in range(1, NZ):
            combined = combined + held[source, r].astype(F32)
        strips[r] = combined.astype(BF16)

    sends = []
    for step in range(1, NY):
        r = lax.rem(y + step, NY)
        copy = pltpu.make_async_remote_copy(
            src_ref=strips.at[r],
            dst_ref=window.at[1 + y],
            send_sem=y_send.at[step],
            recv_sem=y_recv.at[step],
            device_id=device(x, z, core, r),
            device_id_type=MESH,
        )
        copy.start()
        sends.append(copy)

    def edge(r, upper):
        return pltpu.make_async_remote_copy(
            src_ref=strips.at[r - 1 if upper else r + 1],
            dst_ref=window.at[0 if upper else NY + 1],
            send_sem=edge_send.at[r],
            recv_sem=edge_recv.at[0 if upper else 1],
            device_id=device(x, z, core, r),
            device_id_type=MESH,
        )

    @pl.when(y == NY - 1)
    def _():
        for r in range(1, NY - 1):
            edge(r, True).start()
        window[0] = strips[NY - 2]
        window[NY + 1] = jnp.zeros((STRIP, CC * B), BF16)

    @pl.when(y == 0)
    def _():
        for r in range(1, NY - 1):
            edge(r, False).start()
        window[0] = jnp.zeros((STRIP, CC * B), BF16)
        window[NY + 1] = strips[1]

    window[1 + y] = strips[y]
    for copy in sends:
        copy.wait()

    @pl.when((y > 0) & (y < NY - 1))
    def _():
        edge(1, True).wait_recv()
        edge(1, False).wait_recv()

    @pl.when(y == NY - 1)
    def _():
        for r in range(1, NY - 1):
            edge(r, True).wait_send()

    @pl.when(y == 0)
    def _():
        for r in range(1, NY - 1):
            edge(r, False).wait_send()

    for c in range(CC):
        at = slice(c * B, (c + 1) * B)
        padded[:, B + c * B : 2 * B + c * B] = jnp.dot(
            rowf[:, :ROWS], window[:, :, at].reshape(ROWS, B), preferred_element_type=F32
        ).astype(BF16)
    for c in range(CC):
        out_ref[:, c * B : (c + 1) * B] = jnp.dot(
            padded[:, c * B : c * B + 384], colf[...], preferred_element_type=F32
        )


def detect(taps, pieces):
    dma = pltpu.SemaphoreType.DMA
    return pl.pallas_call(
        detect_kernel,
        out_shape=jax.ShapeDtypeStruct((B, CC * B), F32),
        in_specs=[pl.BlockSpec(memory_space=pltpu.SMEM), pl.BlockSpec(memory_space=pl.ANY)],
        out_specs=pl.BlockSpec(memory_space=pltpu.VMEM),
        scratch_shapes=[
            pltpu.VMEM((NZ, CR, STRIP, CC * B), BF16),
            pltpu.VMEM((CR // 2, STRIP, CC * B), BF16),
            pltpu.VMEM((CR, STRIP, CC * B), BF16),
            pltpu.VMEM((NY + 2, STRIP, CC * B), BF16),
            pltpu.VMEM((B, 256), BF16),
            pltpu.VMEM((384, B), BF16),
            pltpu.VMEM((B, (CC + 2) * B), BF16),
            dma((NZ,)),
            dma((NZ,)),
            dma((3,)),
            dma((3,)),
            dma((NY,)),
            dma((NY,)),
            dma((NY,)),
            dma((2,)),
            dma,
        ],
        compiler_params=pltpu.CompilerParams(
            collective_id=1, has_side_effects=True, vmem_limit_bytes=8 * 1024 * 1024
        ),
        name="detect",
    )(taps, pieces)


def ranks(patch):
    earlier = jnp.arange(BLK)[None, :] < jnp.arange(BLK)[:, None]
    same = patch[..., :, None] == patch[..., None, :]
    return jnp.sum((same & earlier).astype(jnp.int32), axis=-1)


def local(
    raw_blocks,
    patch_of_block,
    cell_of_block,
    band_of_block,
    block_weight,
    basis_coef,
    row_basis,
    col_basis,
    band_gain,
    filter_taps,
):
    x, z, core, y = coordinates()
    patch = patch_of_block[:, 0]
    rank = ranks(patch)
    target = band_of_block * CELLS + cell_of_block
    own_details = jnp.stack([v.astype(F32) for v in (patch, target, rank, block_weight)])
    patch_core = patch % NC
    patch_z = patch // NC % NZ
    patch_x = patch // (NC * NZ)
    slot = (patch_x * NC + patch_core) * (NY * SLOTS) + patch_z * CAP + rank
    info, slot = lax.optimization_barrier((own_details.reshape(1, 1, 4 * BLK), slot))
    outgoing = match(slot, basis_coef.astype(F32), row_basis, col_basis, raw_blocks)
    arrived, details = plane_exchange(
        outgoing.reshape(PLANE, SLOTS, STRIP, B), info
    )
    details = details.reshape(NZ, PLANE, 4, BLK)

    my_patches = (x * NZ + jnp.arange(NZ, dtype=jnp.int32)) * NC + core
    every_patch = details[:, :, 0].astype(jnp.int32).reshape(-1)
    every_target = details[:, :, 1].astype(jnp.int32).reshape(-1)
    every_weight = details[:, :, 3].reshape(-1)
    share = jnp.where(every_patch == my_patches[:, None], every_weight, 0.0).astype(BF16)
    hits = (every_target == jnp.arange(TARGETS, dtype=jnp.int32)[:, None]).astype(BF16)
    weight_sum = lax.dot_general(
        share, hits, (((1,), (1,)), ((), ())), preferred_element_type=F32
    )
    gain = (jnp.repeat(band_gain, CELLS) / jnp.maximum(weight_sum, 1.0)).reshape(-1)
    bins = (my_patches[:, None] * TARGETS + jnp.arange(TARGETS, dtype=jnp.int32)).reshape(-1)
    near = lax.dynamic_index_in_dim(details, z, axis=0, keepdims=False)
    near_names = near[:, :3].astype(jnp.int32)
    near_patch, near_target, near_rank = near_names[:, 0], near_names[:, 1], near_names[:, 2]
    near_cell = near_target % CELLS
    near_key = near_patch * TARGETS + near_target
    near_gain = jnp.sum(jnp.where(near_key[..., None] == bins, gain, 0.0), axis=-1)
    near_scale = near_gain * near[:, 3]
    chosen = (near_patch[:, None, None, :] == my_patches[:, None, None]) & (
        near_rank[:, None, None, :] == jnp.arange(CAP, dtype=jnp.int32)[:, None]
    )
    scale = jnp.sum(jnp.where(chosen, near_scale[:, None, None, :], 0.0), axis=-1).reshape(-1)
    cell = jnp.sum(jnp.where(chosen, near_cell[:, None, None, :] + 1, 0), axis=-1).reshape(-1) - 1

    pieces = gather_slots(cell, scale, arrived).reshape(NZ, CR, STRIP, CC * B)
    return detect(filter_taps, pieces)[None]


def solution(mesh):
    return jax.shard_map(
        local,
        mesh=mesh,
        in_specs=(
            P(None, ("sky", "band")),
            P(("sky", "band"), None),
            P(("sky", "band")),
            P(("sky", "band")),
            P(("sky", "band")),
            P(("sky", "band"), None),
            P(),
            P(),
            P(),
            P(),
        ),
        out_specs=P("sky", "band", None),
        check_vma=False,
    )
```

```python
import functools

import jax
import jax.numpy as jnp
from jax import lax
from jax.experimental import pallas as pl
from jax.experimental.pallas import tpu as pltpu
from jax.sharding import PartitionSpec as P

B = 128
TAPS = 41
RADIUS = 20
SIDE = 168
NBASIS = 3
BANDS = 6
CR = 4
CC = 4
CELLS = 16
TARGETS = BANDS * CELLS
BLK = 32
CAP = 2
NX, NZ, NC, NY = 4, 8, 2, 4
PLANE = NX * NC * NY
SLOTS = NZ * CAP
STRIP = B // NY
ROWS = B + 2 * STRIP
MESH = pl.DeviceIdType.MESH
HALFWAY = ((2, 2), (2, 0), (0, 2), (2, 1), (1, 2), (2, 3), (3, 2))
RELAYED = tuple((dx, 1, dy) for dx, dy in HALFWAY)
DIRECT = tuple((dx, 0, dy) for dx, dy in HALFWAY) + tuple(
    (dx, dc, dy)
    for dx, dy in ((1, 3), (3, 1), (1, 1), (3, 3), (1, 0), (3, 0), (0, 1), (0, 3), (0, 0))
    for dc in range(NC)
    if (dx, dc, dy) != (0, 0, 0)
)
F32 = jnp.float32
BF16 = jnp.bfloat16


def coordinates():
    sky = lax.axis_index("sky")
    core = lax.rem(sky, NC)
    z = lax.rem(lax.div(sky, NC), NZ)
    x = lax.div(sky, NC * NZ)
    return x, z, core, lax.axis_index("band")


def device(x, z, core, y):
    return {"sky": (x * NZ + z) * NC + core, "band": y}


def banded(shape, diagonal, taps, rows):
    distance = diagonal(
        lax.broadcasted_iota(jnp.int32, shape, 0), lax.broadcasted_iota(jnp.int32, shape, 1)
    )

    def step(t, held):
        hit = distance == t
        return tuple(jnp.where(hit, taps(k, t), held[k]) for k in range(rows))

    return lax.fori_loop(0, TAPS, step, tuple(jnp.zeros(shape, F32) for _ in range(rows)))


def match_kernel(
    slot_ref, coef_ref, row_ref, col_ref, raw_ref, out_ref, rowk, colk, sectioned
):
    for part in range(0, B, 32):
        stack = banded((32, 256), lambda i, j: j - i - part, lambda k, t: row_ref[k, t], NBASIS)
        for k in range(NBASIS):
            rowk[k * B + part : k * B + part + 32, :] = stack[k].astype(BF16)
    colk[...] = jnp.zeros_like(colk)
    for part in range(0, 192, 64):
        for shift in range(2):
            stack = banded(
                (64, B),
                lambda u, l: u + part - l - 8 * shift,
                lambda k, t: col_ref[k, t],
                NBASIS,
            )
            for k in range(NBASIS):
                colk[shift, k, B + part : B + part + 64, :] = stack[k].astype(BF16)

    def clear(d, _):
        out_ref[pl.ds(d * SLOTS, SLOTS)] = jnp.zeros((SLOTS, STRIP, B), BF16)
        return 0

    lax.fori_loop(0, PLANE, clear, 0)

    def rows(step, _):
        at = pl.ds(pl.multiple_of(step * 256, 256), 256)
        sectioned[:, at] = jnp.dot(
            rowk[:, :SIDE], raw_ref[:, at], preferred_element_type=F32
        ).astype(BF16)
        return 0

    lax.fori_loop(0, BLK * SIDE // 256, rows, 0)

    def columns(group, _):
        for j in range(16):
            first = j * SIDE // B * B
            offset = j * SIDE - first
            width = 256 if offset + SIDE <= 256 else 384
            shift = offset // 8 % 2
            start = B - offset + 8 * shift
            at = pl.ds(pl.multiple_of(group * (16 * SIDE) + first, B), width)
            block = group * 16 + j
            total = None
            for k in range(NBASIS):
                term = coef_ref[block, k] * jnp.dot(
                    sectioned[k * B : (k + 1) * B, at],
                    colk[shift, k, start : start + width, :],
                    preferred_element_type=F32,
                )
                total = term if total is None else total + term
            slot = slot_ref[block]
            for strip in range(NY):
                out_ref[slot + strip * SLOTS] = total[strip * STRIP : (strip + 1) * STRIP].astype(
                    BF16
                )
        return 0

    lax.fori_loop(0, BLK // 16, columns, 0)


def match(slot, coef, row_basis, col_basis, raw):
    smem = pl.BlockSpec(memory_space=pltpu.SMEM)
    vmem = pl.BlockSpec(memory_space=pltpu.VMEM)
    return pl.pallas_call(
        match_kernel,
        out_shape=jax.ShapeDtypeStruct((PLANE * SLOTS, STRIP, B), BF16),
        in_specs=[smem, smem, smem, smem, vmem],
        out_specs=vmem,
        scratch_shapes=[
            pltpu.VMEM((NBASIS * B, 256), BF16),
            pltpu.VMEM((2, NBASIS, 512, B), BF16),
            pltpu.VMEM((NBASIS * B, BLK * SIDE), BF16),
        ],
        compiler_params=pltpu.CompilerParams(vmem_limit_bytes=24 * 1024 * 1024),
        name="match",
    )(slot, coef, row_basis, col_basis, raw)


def offset_id(offset):
    dx, dc, dy = offset
    return (dx * NC + dc) * NY + dy


def plane_kernel(
    out_ref,
    info_ref,
    in_ref,
    every_ref,
    own,
    passing,
    send_sem,
    recv_sem,
    pass_send,
    pass_recv,
    relay_send,
    info_send,
    info_recv,
    z_send,
    z_recv,
    own_sem,
    info_sem,
):
    x, z, core, y = coordinates()
    me = (x * NC + core) * NY + y

    def moved(dx, dc, dy):
        return lax.rem(x + dx, NX), lax.rem(core + dc, NC), lax.rem(y + dy, NY)

    def index(place):
        return (place[0] * NC + place[1]) * NY + place[2]

    def at(place):
        return device(place[0], z, place[1], place[2])

    everyone = RELAYED + DIRECT
    barrier = pltpu.get_barrier_semaphore()
    for offset in everyone:
        pl.semaphore_signal(barrier, inc=1, device_id=at(moved(*offset)), device_id_type=MESH)
    for step in range(1, NZ):
        pl.semaphore_signal(
            barrier,
            inc=1,
            device_id=device(x, lax.rem(z + step, NZ), core, y),
            device_id_type=MESH,
        )
    take = pltpu.make_async_copy(out_ref.at[me], own, own_sem)
    take.start()
    keep = pltpu.make_async_copy(info_ref.at[0], every_ref.at[z, me], info_sem)
    keep.start()
    pl.semaphore_wait(barrier, PLANE - 1 + NZ - 1)
    infos = []
    for offset in everyone:
        copy = pltpu.make_async_remote_copy(
            src_ref=info_ref.at[0],
            dst_ref=every_ref.at[z, me],
            send_sem=info_send.at[offset_id(offset)],
            recv_sem=info_recv.at[offset_id(offset)],
            device_id=at(moved(*offset)),
            device_id_type=MESH,
        )
        copy.start()
        infos.append(copy)
    firsts = []
    edge_x = NX - 1 - lax.rem(x, 2) * (NX - 1)
    edge_y = NY - 1 - lax.rem(y, 2) * (NY - 1)
    for k, (dx, dc, dy) in enumerate(RELAYED):
        over_x, over_y = dx == 2, dy == 2
        hold = k * 4
        if over_x:
            hold = hold + lax.div(x, 2) * 2
        if over_y:
            hold = hold + lax.div(y, 2)
        copy = pltpu.make_async_remote_copy(
            src_ref=out_ref.at[index(moved(dx, dc, dy))],
            dst_ref=passing.at[hold],
            send_sem=pass_send.at[k],
            recv_sem=pass_recv.at[hold],
            device_id=at((edge_x if over_x else x, core, edge_y if over_y else y)),
            device_id_type=MESH,
        )
        copy.start()
        firsts.append(copy)
    copies = []

    def send(offset):
        copy = pltpu.make_async_remote_copy(
            src_ref=out_ref.at[index(moved(*offset))],
            dst_ref=in_ref.at[me],
            send_sem=send_sem.at[offset_id(offset)],
            recv_sem=recv_sem.at[offset_id(offset)],
            device_id=at(moved(*offset)),
            device_id_type=MESH,
        )
        copy.start()
        copies.append(copy)

    for offset in DIRECT:
        send(offset)
    take.wait()
    put = pltpu.make_async_copy(own, in_ref.at[me], own_sem)
    put.start()
    def relay(k, jx, jy):
        dx, dc, dy = RELAYED[k]
        hold = k * 4 + jx * 2 + jy
        from_x = jx * 2 + 1 - lax.div(x, NX - 1) if dx == 2 else x
        from_y = jy * 2 + 1 - lax.div(y, NY - 1) if dy == 2 else y
        dest = (lax.rem(from_x + dx, NX), lax.rem(core + dc, NC), lax.rem(from_y + dy, NY))
        return pltpu.make_async_remote_copy(
            src_ref=passing.at[hold],
            dst_ref=in_ref.at[index((from_x, core, from_y))],
            send_sem=relay_send.at[hold],
            recv_sem=recv_sem.at[offset_id(RELAYED[k])],
            device_id=at(dest),
            device_id_type=MESH,
        )

    def arrival(k, jx, jy):
        hold = k * 4 + jx * 2 + jy
        return pltpu.make_async_remote_copy(
            src_ref=out_ref.at[0],
            dst_ref=passing.at[hold],
            send_sem=pass_send.at[k],
            recv_sem=pass_recv.at[hold],
            device_id=at(moved(1, 0, 0)),
            device_id_type=MESH,
        )

    def relays(act):
        for k, (dx, dc, dy) in enumerate(RELAYED):
            over_x, over_y = dx == 2, dy == 2
            here_x = (x == 0) | (x == NX - 1)
            here_y = (y == 0) | (y == NY - 1)
            here = here_x & here_y if over_x and over_y else here_x if over_x else here_y

            @pl.when(here)
            def _():
                for jx in range(2 if over_x else 1):
                    for jy in range(2 if over_y else 1):
                        act(k, jx, jy)

    def forward(k, jx, jy):
        arrival(k, jx, jy).wait_recv()
        relay(k, jx, jy).start()

    relays(forward)
    keep.wait()
    for copy in infos:
        copy.wait()
    planes = []
    for step in range(1, NZ):
        copy = pltpu.make_async_remote_copy(
            src_ref=every_ref.at[z],
            dst_ref=every_ref.at[z],
            send_sem=z_send.at[step],
            recv_sem=z_recv.at[step],
            device_id=device(x, lax.rem(z + step, NZ), core, y),
            device_id_type=MESH,
        )
        copy.start()
        planes.append(copy)
    put.wait()
    for copy in planes:
        copy.wait()
    for copy in firsts:
        copy.wait_send()
    relays(lambda k, jx, jy: relay(k, jx, jy).wait_send())
    for offset in RELAYED:
        pltpu.make_async_remote_copy(
            src_ref=out_ref.at[0],
            dst_ref=in_ref.at[index(moved(NX - offset[0], NC - offset[1], NY - offset[2]))],
            send_sem=send_sem.at[0],
            recv_sem=recv_sem.at[offset_id(offset)],
            device_id=at(moved(1, 0, 0)),
            device_id_type=MESH,
        ).wait_recv()
    for copy in copies:
        copy.wait()


def plane_exchange(outgoing, info):
    hbm = pl.BlockSpec(memory_space=pl.ANY)
    vmem = pl.BlockSpec(memory_space=pltpu.VMEM)
    dma = pltpu.SemaphoreType.DMA
    return pl.pallas_call(
        plane_kernel,
        out_shape=(
            jax.ShapeDtypeStruct((PLANE, SLOTS, STRIP, B), BF16),
            jax.ShapeDtypeStruct((NZ, PLANE, 1, B), F32),
        ),
        in_specs=[hbm, vmem],
        out_specs=(pl.BlockSpec(memory_space=pltpu.HBM), vmem),
        scratch_shapes=[
            pltpu.VMEM((SLOTS, STRIP, B), BF16),
            pltpu.VMEM((4 * len(RELAYED), SLOTS, STRIP, B), BF16),
            dma((PLANE,)),
            dma((PLANE,)),
            dma((len(RELAYED),)),
            dma((4 * len(RELAYED),)),
            dma((4 * len(RELAYED),)),
            dma((PLANE,)),
            dma((PLANE,)),
            dma((NZ,)),
            dma((NZ,)),
            dma,
            dma,
        ],
        compiler_params=pltpu.CompilerParams(
            collective_id=0, has_side_effects=True, vmem_limit_bytes=8 * 1024 * 1024
        ),
        name="plane_exchange",
    )(outgoing, info)


def gather_kernel(cell_ref, scale_ref, in_ref, out_ref, total):
    step = pl.program_id(0)
    per_step = in_ref.shape[0]

    @pl.when(step == 0)
    def _():
        def clear(i, _):
            total[i] = jnp.zeros((STRIP, CC * B), F32)
            return 0

        lax.fori_loop(0, NZ * CR, clear, 0)

    for d in range(per_step):
        for s in range(SLOTS):
            slot = (step * per_step + d) * SLOTS + s
            cell = cell_ref[slot]

            @pl.when(cell >= 0)
            def _():
                row = (s // CAP) * CR + lax.div(cell, CC)
                column = pl.multiple_of(lax.rem(cell, CC) * B, B)
                total[row, :, pl.ds(column, B)] += scale_ref[slot] * in_ref[d, s].astype(F32)

    @pl.when(step == pl.num_programs(0) - 1)
    def _():
        def write(i, _):
            out_ref[i] = total[i].astype(BF16)
            return 0

        lax.fori_loop(0, NZ * CR, write, 0)


def gather_slots(cell, scale, arrived):
    smem = pl.BlockSpec(memory_space=pltpu.SMEM)
    per_step = 4
    shape = (NZ * CR, STRIP, CC * B)
    return pl.pallas_call(
        gather_kernel,
        grid=(PLANE // per_step,),
        out_shape=jax.ShapeDtypeStruct(shape, BF16),
        in_specs=[smem, smem, pl.BlockSpec((per_step, SLOTS, STRIP, B), lambda i: (i, 0, 0, 0))],
        out_specs=pl.BlockSpec(shape, lambda i: (0, 0, 0)),
        scratch_shapes=[pltpu.VMEM(shape, F32)],
        compiler_params=pltpu.CompilerParams(vmem_limit_bytes=16 * 1024 * 1024),
        name="gather_slots",
    )(cell, scale, arrived)


def detect_kernel(
    taps_ref,
    piece_ref,
    out_ref,
    held,
    passing,
    strips,
    window,
    rowf,
    colf,
    padded,
    z_send,
    z_recv,
    far_send,
    far_recv,
    y_send,
    y_recv,
    edge_send,
    edge_recv,
    own_sem,
):
    x, z, core, y = coordinates()
    barrier = pltpu.get_barrier_semaphore()
    for step in range(1, NZ):
        pl.semaphore_signal(
            barrier,
            inc=1,
            device_id=device(x, lax.rem(z + step, NZ), core, y),
            device_id_type=MESH,
        )
    for step in range(1, NY):
        pl.semaphore_signal(
            barrier,
            inc=1,
            device_id=device(x, z, core, lax.rem(y + step, NY)),
            device_id_type=MESH,
        )
    keep = pltpu.make_async_copy(piece_ref.at[z], held.at[z], own_sem)
    keep.start()
    pl.semaphore_wait(barrier, NZ - 1 + NY - 1)
    pieces = []
    half = CR // 2
    far = lax.rem(z + NZ // 2, NZ)
    first = pltpu.make_async_remote_copy(
        src_ref=piece_ref.at[far, pl.ds(half, half)],
        dst_ref=passing,
        send_sem=far_send.at[0],
        recv_sem=far_recv.at[0],
        device_id=device(x, lax.rem(z + NZ - 1, NZ), core, y),
        device_id_type=MESH,
    )
    first.start()
    direct = pltpu.make_async_remote_copy(
        src_ref=piece_ref.at[far, pl.ds(0, half)],
        dst_ref=held.at[z, pl.ds(0, half)],
        send_sem=far_send.at[1],
        recv_sem=far_recv.at[1],
        device_id=device(x, far, core, y),
        device_id_type=MESH,
    )
    direct.start()
    pieces.append(direct)

    def send(step):
        peer = lax.rem(z + step, NZ)
        copy = pltpu.make_async_remote_copy(
            src_ref=piece_ref.at[peer],
            dst_ref=held.at[z],
            send_sem=z_send.at[step],
            recv_sem=z_recv.at[step],
            device_id=device(x, peer, core, y),
            device_id_type=MESH,
        )
        copy.start()
        pieces.append(copy)

    for step in (3, 2, 1, 7):
        send(step)
    first.wait_recv()
    second = pltpu.make_async_remote_copy(
        src_ref=passing,
        dst_ref=held.at[lax.rem(z + 1, NZ), pl.ds(half, half)],
        send_sem=far_send.at[2],
        recv_sem=far_recv.at[2],
        device_id=device(x, lax.rem(z + 1 + NZ // 2, NZ), core, y),
        device_id_type=MESH,
    )
    second.start()
    pieces.append(second)
    for step in (5, 6):
        send(step)

    def tap(k, t):
        return taps_ref[t]

    for part in range(0, B, 32):
        rowf[part : part + 32, :] = banded(
            (32, 256), lambda i, u: u - i - part - (STRIP - RADIUS), tap, 1
        )[0].astype(BF16)
    for part in range(0, 384, 64):
        colf[part : part + 64, :] = banded(
            (64, B), lambda m, l: m + part - B - l + RADIUS, tap, 1
        )[0].astype(BF16)
    padded[:, :B] = jnp.zeros((B, B), BF16)
    padded[:, B + CC * B :] = jnp.zeros((B, B), BF16)

    keep.wait()
    first.wait_send()
    for copy in pieces:
        copy.wait()
    for r in range(CR):
        combined = held[0, r].astype(F32)
        for source in range(1, NZ):
            combined = combined + held[source, r].astype(F32)
        strips[r] = combined.astype(BF16)

    sends = []
    for step in range(1, NY):
        r = lax.rem(y + step, NY)
        copy = pltpu.make_async_remote_copy(
            src_ref=strips.at[r],
            dst_ref=window.at[1 + y],
            send_sem=y_send.at[step],
            recv_sem=y_recv.at[step],
            device_id=device(x, z, core, r),
            device_id_type=MESH,
        )
        copy.start()
        sends.append(copy)

    def edge(r, upper):
        return pltpu.make_async_remote_copy(
            src_ref=strips.at[r - 1 if upper else r + 1],
            dst_ref=window.at[0 if upper else NY + 1],
            send_sem=edge_send.at[r],
            recv_sem=edge_recv.at[0 if upper else 1],
            device_id=device(x, z, core, r),
            device_id_type=MESH,
        )

    @pl.when(y == NY - 1)
    def _():
        for r in range(1, NY - 1):
            edge(r, True).start()
        window[0] = strips[NY - 2]
        window[NY + 1] = jnp.zeros((STRIP, CC * B), BF16)

    @pl.when(y == 0)
    def _():
        for r in range(1, NY - 1):
            edge(r, False).start()
        window[0] = jnp.zeros((STRIP, CC * B), BF16)
        window[NY + 1] = strips[1]

    window[1 + y] = strips[y]
    for copy in sends:
        copy.wait()

    @pl.when((y > 0) & (y < NY - 1))
    def _():
        edge(1, True).wait_recv()
        edge(1, False).wait_recv()

    @pl.when(y == NY - 1)
    def _():
        for r in range(1, NY - 1):
            edge(r, True).wait_send()

    @pl.when(y == 0)
    def _():
        for r in range(1, NY - 1):
            edge(r, False).wait_send()

    for c in range(CC):
        at = slice(c * B, (c + 1) * B)
        padded[:, B + c * B : 2 * B + c * B] = jnp.dot(
            rowf[:, :ROWS], window[:, :, at].reshape(ROWS, B), preferred_element_type=F32
        ).astype(BF16)
    for c in range(CC):
        out_ref[:, c * B : (c + 1) * B] = jnp.dot(
            padded[:, c * B : c * B + 384], colf[...], preferred_element_type=F32
        )


def detect(taps, pieces):
    dma = pltpu.SemaphoreType.DMA
    return pl.pallas_call(
        detect_kernel,
        out_shape=jax.ShapeDtypeStruct((B, CC * B), F32),
        in_specs=[pl.BlockSpec(memory_space=pltpu.SMEM), pl.BlockSpec(memory_space=pl.ANY)],
        out_specs=pl.BlockSpec(memory_space=pltpu.VMEM),
        scratch_shapes=[
            pltpu.VMEM((NZ, CR, STRIP, CC * B), BF16),
            pltpu.VMEM((CR // 2, STRIP, CC * B), BF16),
            pltpu.VMEM((CR, STRIP, CC * B), BF16),
            pltpu.VMEM((NY + 2, STRIP, CC * B), BF16),
            pltpu.VMEM((B, 256), BF16),
            pltpu.VMEM((384, B), BF16),
            pltpu.VMEM((B, (CC + 2) * B), BF16),
            dma((NZ,)),
            dma((NZ,)),
            dma((3,)),
            dma((3,)),
            dma((NY,)),
            dma((NY,)),
            dma((NY,)),
            dma((2,)),
            dma,
        ],
        compiler_params=pltpu.CompilerParams(
            collective_id=1, has_side_effects=True, vmem_limit_bytes=8 * 1024 * 1024
        ),
        name="detect",
    )(taps, pieces)


def ranks(patch):
    earlier = jnp.arange(BLK)[None, :] < jnp.arange(BLK)[:, None]
    same = patch[..., :, None] == patch[..., None, :]
    return jnp.sum((same & earlier).astype(jnp.int32), axis=-1)


def local(
    raw_blocks,
    patch_of_block,
    cell_of_block,
    band_of_block,
    block_weight,
    basis_coef,
    row_basis,
    col_basis,
    band_gain,
    filter_taps,
):
    x, z, core, y = coordinates()
    patch = patch_of_block[:, 0]
    rank = ranks(patch)
    target = band_of_block * CELLS + cell_of_block
    own_details = jnp.stack([v.astype(F32) for v in (patch, target, rank, block_weight)])
    patch_core = patch % NC
    patch_z = patch // NC % NZ
    patch_x = patch // (NC * NZ)
    slot = (patch_x * NC + patch_core) * (NY * SLOTS) + patch_z * CAP + rank
    info, slot = lax.optimization_barrier((own_details.reshape(1, 1, 4 * BLK), slot))
    outgoing = match(slot, basis_coef.astype(F32), row_basis, col_basis, raw_blocks)
    arrived, details = plane_exchange(
        outgoing.reshape(PLANE, SLOTS, STRIP, B), info
    )
    details = details.reshape(NZ, PLANE, 4, BLK)

    my_patches = (x * NZ + jnp.arange(NZ, dtype=jnp.int32)) * NC + core
    every_patch = details[:, :, 0].astype(jnp.int32).reshape(-1)
    every_target = details[:, :, 1].astype(jnp.int32).reshape(-1)
    every_weight = details[:, :, 3].reshape(-1)
    share = jnp.where(every_patch == my_patches[:, None], every_weight, 0.0).astype(BF16)
    hits = (every_target == jnp.arange(TARGETS, dtype=jnp.int32)[:, None]).astype(BF16)
    weight_sum = lax.dot_general(
        share, hits, (((1,), (1,)), ((), ())), preferred_element_type=F32
    )
    gain = (jnp.repeat(band_gain, CELLS) / jnp.maximum(weight_sum, 1.0)).reshape(-1)
    bins = (my_patches[:, None] * TARGETS + jnp.arange(TARGETS, dtype=jnp.int32)).reshape(-1)
    near = lax.dynamic_index_in_dim(details, z, axis=0, keepdims=False)
    near_names = near[:, :3].astype(jnp.int32)
    near_patch, near_target, near_rank = near_names[:, 0], near_names[:, 1], near_names[:, 2]
    near_cell = near_target % CELLS
    near_key = near_patch * TARGETS + near_target
    near_gain = jnp.sum(jnp.where(near_key[..., None] == bins, gain, 0.0), axis=-1)
    near_scale = near_gain * near[:, 3]
    chosen = (near_patch[:, None, None, :] == my_patches[:, None, None]) & (
        near_rank[:, None, None, :] == jnp.arange(CAP, dtype=jnp.int32)[:, None]
    )
    scale = jnp.sum(jnp.where(chosen, near_scale[:, None, None, :], 0.0), axis=-1).reshape(-1)
    cell = jnp.sum(jnp.where(chosen, near_cell[:, None, None, :] + 1, 0), axis=-1).reshape(-1) - 1

    pieces = gather_slots(cell, scale, arrived).reshape(NZ, CR, STRIP, CC * B)
    return detect(filter_taps, pieces)[None]


def solution(mesh):
    return jax.shard_map(
        local,
        mesh=mesh,
        in_specs=(
            P(None, ("sky", "band")),
            P(("sky", "band"), None),
            P(("sky", "band")),
            P(("sky", "band")),
            P(("sky", "band")),
            P(("sky", "band"), None),
            P(),
            P(),
            P(),
            P(),
        ),
        out_specs=P("sky", "band", None),
        check_vma=False,
    )
```

```python
import functools

import jax
import jax.numpy as jnp
from jax import lax
from jax.experimental import pallas as pl
from jax.experimental.pallas import tpu as pltpu
from jax.sharding import PartitionSpec as P

B = 128
TAPS = 41
RADIUS = 20
SIDE = 168
NBASIS = 3
BANDS = 6
CR = 4
CC = 4
CELLS = 16
TARGETS = BANDS * CELLS
BLK = 32
CAP = 2
NX, NZ, NC, NY = 4, 8, 2, 4
PLANE = NX * NC * NY
SLOTS = NZ * CAP
STRIP = B // NY
ROWS = B + 2 * STRIP
MESH = pl.DeviceIdType.MESH
HALFWAY = ((2, 2), (2, 0), (0, 2), (2, 1), (1, 2), (2, 3), (3, 2))
RELAYED = tuple((dx, 1, dy) for dx, dy in HALFWAY)
DIRECT = tuple((dx, 0, dy) for dx, dy in HALFWAY) + tuple(
    (dx, dc, dy)
    for dx, dy in ((1, 3), (3, 1), (1, 1), (3, 3), (1, 0), (3, 0), (0, 1), (0, 3), (0, 0))
    for dc in range(NC)
    if (dx, dc, dy) != (0, 0, 0)
)
F32 = jnp.float32
BF16 = jnp.bfloat16


def coordinates():
    sky = lax.axis_index("sky")
    core = lax.rem(sky, NC)
    z = lax.rem(lax.div(sky, NC), NZ)
    x = lax.div(sky, NC * NZ)
    return x, z, core, lax.axis_index("band")


def device(x, z, core, y):
    return {"sky": (x * NZ + z) * NC + core, "band": y}


def banded(shape, diagonal, taps, rows):
    distance = diagonal(
        lax.broadcasted_iota(jnp.int32, shape, 0), lax.broadcasted_iota(jnp.int32, shape, 1)
    )

    def step(t, held):
        hit = distance == t
        return tuple(jnp.where(hit, taps(k, t), held[k]) for k in range(rows))

    return lax.fori_loop(0, TAPS, step, tuple(jnp.zeros(shape, F32) for _ in range(rows)))


def match_kernel(
    slot_ref, coef_ref, row_ref, col_ref, raw_ref, out_ref, rowk, colk, sectioned
):
    for part in range(0, B, 32):
        stack = banded((32, 256), lambda i, j: j - i - part, lambda k, t: row_ref[k, t], NBASIS)
        for k in range(NBASIS):
            rowk[k * B + part : k * B + part + 32, :] = stack[k].astype(BF16)
    colk[...] = jnp.zeros_like(colk)
    for part in range(0, 192, 64):
        for shift in range(2):
            stack = banded(
                (64, B),
                lambda u, l: u + part - l - 8 * shift,
                lambda k, t: col_ref[k, t],
                NBASIS,
            )
            for k in range(NBASIS):
                colk[shift, k, B + part : B + part + 64, :] = stack[k].astype(BF16)

    def clear(d, _):
        out_ref[pl.ds(d * SLOTS, SLOTS)] = jnp.zeros((SLOTS, STRIP, B), BF16)
        return 0

    lax.fori_loop(0, PLANE, clear, 0)

    def rows(step, _):
        at = pl.ds(pl.multiple_of(step * 256, 256), 256)
        sectioned[:, at] = jnp.dot(
            rowk[:, :SIDE], raw_ref[:, at], preferred_element_type=F32
        ).astype(BF16)
        return 0

    lax.fori_loop(0, BLK * SIDE // 256, rows, 0)

    def columns(group, _):
        for j in range(16):
            first = j * SIDE // B * B
            offset = j * SIDE - first
            width = 256 if offset + SIDE <= 256 else 384
            shift = offset // 8 % 2
            start = B - offset + 8 * shift
            at = pl.ds(pl.multiple_of(group * (16 * SIDE) + first, B), width)
            block = group * 16 + j
            total = None
            for k in range(NBASIS):
                term = coef_ref[block, k] * jnp.dot(
                    sectioned[k * B : (k + 1) * B, at],
                    colk[shift, k, start : start + width, :],
                    preferred_element_type=F32,
                )
                total = term if total is None else total + term
            slot = slot_ref[block]
            for strip in range(NY):
                out_ref[slot + strip * SLOTS] = total[strip * STRIP : (strip + 1) * STRIP].astype(
                    BF16
                )
        return 0

    lax.fori_loop(0, BLK // 16, columns, 0)


def match(slot, coef, row_basis, col_basis, raw):
    smem = pl.BlockSpec(memory_space=pltpu.SMEM)
    vmem = pl.BlockSpec(memory_space=pltpu.VMEM)
    return pl.pallas_call(
        match_kernel,
        out_shape=jax.ShapeDtypeStruct((PLANE * SLOTS, STRIP, B), BF16),
        in_specs=[smem, smem, smem, smem, vmem],
        out_specs=vmem,
        scratch_shapes=[
            pltpu.VMEM((NBASIS * B, 256), BF16),
            pltpu.VMEM((2, NBASIS, 512, B), BF16),
            pltpu.VMEM((NBASIS * B, BLK * SIDE), BF16),
        ],
        compiler_params=pltpu.CompilerParams(vmem_limit_bytes=24 * 1024 * 1024),
        name="match",
    )(slot, coef, row_basis, col_basis, raw)


def offset_id(offset):
    dx, dc, dy = offset
    return (dx * NC + dc) * NY + dy


def plane_kernel(
    out_ref,
    info_ref,
    in_ref,
    every_ref,
    own,
    passing,
    send_sem,
    recv_sem,
    pass_send,
    pass_recv,
    info_send,
    info_recv,
    z_send,
    z_recv,
    own_sem,
    info_sem,
):
    x, z, core, y = coordinates()
    me = (x * NC + core) * NY + y

    def moved(dx, dc, dy):
        return lax.rem(x + dx, NX), lax.rem(core + dc, NC), lax.rem(y + dy, NY)

    def index(place):
        return (place[0] * NC + place[1]) * NY + place[2]

    def at(place):
        return device(place[0], z, place[1], place[2])

    everyone = RELAYED + DIRECT
    barrier = pltpu.get_barrier_semaphore()
    for offset in everyone:
        pl.semaphore_signal(barrier, inc=1, device_id=at(moved(*offset)), device_id_type=MESH)
    for step in range(1, NZ):
        pl.semaphore_signal(
            barrier,
            inc=1,
            device_id=device(x, lax.rem(z + step, NZ), core, y),
            device_id_type=MESH,
        )
    take = pltpu.make_async_copy(out_ref.at[me], own, own_sem)
    take.start()
    keep = pltpu.make_async_copy(info_ref.at[0], every_ref.at[z, me], info_sem)
    keep.start()
    pl.semaphore_wait(barrier, PLANE - 1 + NZ - 1)
    infos = []
    for offset in everyone:
        copy = pltpu.make_async_remote_copy(
            src_ref=info_ref.at[0],
            dst_ref=every_ref.at[z, me],
            send_sem=info_send.at[offset_id(offset)],
            recv_sem=info_recv.at[offset_id(offset)],
            device_id=at(moved(*offset)),
            device_id_type=MESH,
        )
        copy.start()
        infos.append(copy)
    firsts = []
    for k, (dx, dc, dy) in enumerate(RELAYED):
        back_x, back_y = (NX - 1) * (dx == 2), (NY - 1) * (dy == 2)
        copy = pltpu.make_async_remote_copy(
            src_ref=out_ref.at[index(moved(dx, dc, dy))],
            dst_ref=passing.at[k],
            send_sem=pass_send.at[k],
            recv_sem=pass_recv.at[k],
            device_id=at(moved(back_x, 0, back_y)),
            device_id_type=MESH,
        )
        copy.start()
        firsts.append(copy)
    copies = []

    def send(offset):
        copy = pltpu.make_async_remote_copy(
            src_ref=out_ref.at[index(moved(*offset))],
            dst_ref=in_ref.at[me],
            send_sem=send_sem.at[offset_id(offset)],
            recv_sem=recv_sem.at[offset_id(offset)],
            device_id=at(moved(*offset)),
            device_id_type=MESH,
        )
        copy.start()
        copies.append(copy)

    for offset in DIRECT:
        send(offset)
    take.wait()
    put = pltpu.make_async_copy(own, in_ref.at[me], own_sem)
    put.start()
    for k, offset in enumerate(RELAYED):
        dx, dc, dy = offset
        ahead_x, ahead_y = dx == 2, dy == 2
        firsts[k].wait_recv()
        copy = pltpu.make_async_remote_copy(
            src_ref=passing.at[k],
            dst_ref=in_ref.at[index(moved(int(ahead_x), 0, int(ahead_y)))],
            send_sem=send_sem.at[offset_id(offset)],
            recv_sem=recv_sem.at[offset_id(offset)],
            device_id=at(moved((dx + ahead_x) % NX, dc, (dy + ahead_y) % NY)),
            device_id_type=MESH,
        )
        copy.start()
        copies.append(copy)
    keep.wait()
    for copy in infos:
        copy.wait()
    planes = []
    for step in range(1, NZ):
        copy = pltpu.make_async_remote_copy(
            src_ref=every_ref.at[z],
            dst_ref=every_ref.at[z],
            send_sem=z_send.at[step],
            recv_sem=z_recv.at[step],
            device_id=device(x, lax.rem(z + step, NZ), core, y),
            device_id_type=MESH,
        )
        copy.start()
        planes.append(copy)
    put.wait()
    for copy in planes:
        copy.wait()
    for copy in firsts:
        copy.wait_send()
    for copy in copies:
        copy.wait()


def plane_exchange(outgoing, info):
    hbm = pl.BlockSpec(memory_space=pl.ANY)
    vmem = pl.BlockSpec(memory_space=pltpu.VMEM)
    dma = pltpu.SemaphoreType.DMA
    return pl.pallas_call(
        plane_kernel,
        out_shape=(
            jax.ShapeDtypeStruct((PLANE, SLOTS, STRIP, B), BF16),
            jax.ShapeDtypeStruct((NZ, PLANE, 1, B), F32),
        ),
        in_specs=[hbm, vmem],
        out_specs=(pl.BlockSpec(memory_space=pltpu.HBM), vmem),
        scratch_shapes=[
            pltpu.VMEM((SLOTS, STRIP, B), BF16),
            pltpu.VMEM((len(RELAYED), SLOTS, STRIP, B), BF16),
            dma((PLANE,)),
            dma((PLANE,)),
            dma((len(RELAYED),)),
            dma((len(RELAYED),)),
            dma((PLANE,)),
            dma((PLANE,)),
            dma((NZ,)),
            dma((NZ,)),
            dma,
            dma,
        ],
        compiler_params=pltpu.CompilerParams(
            collective_id=0, has_side_effects=True, vmem_limit_bytes=4 * 1024 * 1024
        ),
        name="plane_exchange",
    )(outgoing, info)


def gather_kernel(cell_ref, scale_ref, in_ref, out_ref, total):
    step = pl.program_id(0)
    per_step = in_ref.shape[0]

    @pl.when(step == 0)
    def _():
        def clear(i, _):
            total[i] = jnp.zeros((STRIP, CC * B), F32)
            return 0

        lax.fori_loop(0, NZ * CR, clear, 0)

    for d in range(per_step):
        for s in range(SLOTS):
            slot = (step * per_step + d) * SLOTS + s
            cell = cell_ref[slot]

            @pl.when(cell >= 0)
            def _():
                row = (s // CAP) * CR + lax.div(cell, CC)
                column = pl.multiple_of(lax.rem(cell, CC) * B, B)
                total[row, :, pl.ds(column, B)] += scale_ref[slot] * in_ref[d, s].astype(F32)

    @pl.when(step == pl.num_programs(0) - 1)
    def _():
        def write(i, _):
            out_ref[i] = total[i].astype(BF16)
            return 0

        lax.fori_loop(0, NZ * CR, write, 0)


def gather_slots(cell, scale, arrived):
    smem = pl.BlockSpec(memory_space=pltpu.SMEM)
    per_step = 4
    shape = (NZ * CR, STRIP, CC * B)
    return pl.pallas_call(
        gather_kernel,
        grid=(PLANE // per_step,),
        out_shape=jax.ShapeDtypeStruct(shape, BF16),
        in_specs=[smem, smem, pl.BlockSpec((per_step, SLOTS, STRIP, B), lambda i: (i, 0, 0, 0))],
        out_specs=pl.BlockSpec(shape, lambda i: (0, 0, 0)),
        scratch_shapes=[pltpu.VMEM(shape, F32)],
        compiler_params=pltpu.CompilerParams(vmem_limit_bytes=16 * 1024 * 1024),
        name="gather_slots",
    )(cell, scale, arrived)


def detect_kernel(
    taps_ref,
    piece_ref,
    out_ref,
    held,
    passing,
    strips,
    window,
    rowf,
    colf,
    padded,
    z_send,
    z_recv,
    far_send,
    far_recv,
    y_send,
    y_recv,
    edge_send,
    edge_recv,
    own_sem,
):
    x, z, core, y = coordinates()
    barrier = pltpu.get_barrier_semaphore()
    for step in range(1, NZ):
        pl.semaphore_signal(
            barrier,
            inc=1,
            device_id=device(x, lax.rem(z + step, NZ), core, y),
            device_id_type=MESH,
        )
    for step in range(1, NY):
        pl.semaphore_signal(
            barrier,
            inc=1,
            device_id=device(x, z, core, lax.rem(y + step, NY)),
            device_id_type=MESH,
        )
    keep = pltpu.make_async_copy(piece_ref.at[z], held.at[z], own_sem)
    keep.start()
    pl.semaphore_wait(barrier, NZ - 1 + NY - 1)
    pieces = []
    half = CR // 2
    far = lax.rem(z + NZ // 2, NZ)
    first = pltpu.make_async_remote_copy(
        src_ref=piece_ref.at[far, pl.ds(half, half)],
        dst_ref=passing,
        send_sem=far_send.at[0],
        recv_sem=far_recv.at[0],
        device_id=device(x, lax.rem(z + NZ - 1, NZ), core, y),
        device_id_type=MESH,
    )
    first.start()
    direct = pltpu.make_async_remote_copy(
        src_ref=piece_ref.at[far, pl.ds(0, half)],
        dst_ref=held.at[z, pl.ds(0, half)],
        send_sem=far_send.at[1],
        recv_sem=far_recv.at[1],
        device_id=device(x, far, core, y),
        device_id_type=MESH,
    )
    direct.start()
    pieces.append(direct)

    def send(step):
        peer = lax.rem(z + step, NZ)
        copy = pltpu.make_async_remote_copy(
            src_ref=piece_ref.at[peer],
            dst_ref=held.at[z],
            send_sem=z_send.at[step],
            recv_sem=z_recv.at[step],
            device_id=device(x, peer, core, y),
            device_id_type=MESH,
        )
        copy.start()
        pieces.append(copy)

    for step in (3, 2, 1, 7):
        send(step)
    first.wait_recv()
    second = pltpu.make_async_remote_copy(
        src_ref=passing,
        dst_ref=held.at[lax.rem(z + 1, NZ), pl.ds(half, half)],
        send_sem=far_send.at[2],
        recv_sem=far_recv.at[2],
        device_id=device(x, lax.rem(z + 1 + NZ // 2, NZ), core, y),
        device_id_type=MESH,
    )
    second.start()
    pieces.append(second)
    for step in (5, 6):
        send(step)

    def tap(k, t):
        return taps_ref[t]

    for part in range(0, B, 32):
        rowf[part : part + 32, :] = banded(
            (32, 256), lambda i, u: u - i - part - (STRIP - RADIUS), tap, 1
        )[0].astype(BF16)
    for part in range(0, 384, 64):
        colf[part : part + 64, :] = banded(
            (64, B), lambda m, l: m + part - B - l + RADIUS, tap, 1
        )[0].astype(BF16)
    padded[:, :B] = jnp.zeros((B, B), BF16)
    padded[:, B + CC * B :] = jnp.zeros((B, B), BF16)

    keep.wait()
    first.wait_send()
    for copy in pieces:
        copy.wait()
    for r in range(CR):
        combined = held[0, r].astype(F32)
        for source in range(1, NZ):
            combined = combined + held[source, r].astype(F32)
        strips[r] = combined.astype(BF16)

    sends = []
    for step in range(1, NY):
        r = lax.rem(y + step, NY)
        copy = pltpu.make_async_remote_copy(
            src_ref=strips.at[r],
            dst_ref=window.at[1 + y],
            send_sem=y_send.at[step],
            recv_sem=y_recv.at[step],
            device_id=device(x, z, core, r),
            device_id_type=MESH,
        )
        copy.start()
        sends.append(copy)

    def edge(r, upper):
        return pltpu.make_async_remote_copy(
            src_ref=strips.at[r - 1 if upper else r + 1],
            dst_ref=window.at[0 if upper else NY + 1],
            send_sem=edge_send.at[r],
            recv_sem=edge_recv.at[0 if upper else 1],
            device_id=device(x, z, core, r),
            device_id_type=MESH,
        )

    @pl.when(y == NY - 1)
    def _():
        for r in range(1, NY - 1):
            edge(r, True).start()
        window[0] = strips[NY - 2]
        window[NY + 1] = jnp.zeros((STRIP, CC * B), BF16)

    @pl.when(y == 0)
    def _():
        for r in range(1, NY - 1):
            edge(r, False).start()
        window[0] = jnp.zeros((STRIP, CC * B), BF16)
        window[NY + 1] = strips[1]

    window[1 + y] = strips[y]
    for copy in sends:
        copy.wait()

    @pl.when((y > 0) & (y < NY - 1))
    def _():
        edge(1, True).wait_recv()
        edge(1, False).wait_recv()

    @pl.when(y == NY - 1)
    def _():
        for r in range(1, NY - 1):
            edge(r, True).wait_send()

    @pl.when(y == 0)
    def _():
        for r in range(1, NY - 1):
            edge(r, False).wait_send()

    for c in range(CC):
        at = slice(c * B, (c + 1) * B)
        padded[:, B + c * B : 2 * B + c * B] = jnp.dot(
            rowf[:, :ROWS], window[:, :, at].reshape(ROWS, B), preferred_element_type=F32
        ).astype(BF16)
    for c in range(CC):
        out_ref[:, c * B : (c + 1) * B] = jnp.dot(
            padded[:, c * B : c * B + 384], colf[...], preferred_element_type=F32
        )


def detect(taps, pieces):
    dma = pltpu.SemaphoreType.DMA
    return pl.pallas_call(
        detect_kernel,
        out_shape=jax.ShapeDtypeStruct((B, CC * B), F32),
        in_specs=[pl.BlockSpec(memory_space=pltpu.SMEM), pl.BlockSpec(memory_space=pl.ANY)],
        out_specs=pl.BlockSpec(memory_space=pltpu.VMEM),
        scratch_shapes=[
            pltpu.VMEM((NZ, CR, STRIP, CC * B), BF16),
            pltpu.VMEM((CR // 2, STRIP, CC * B), BF16),
            pltpu.VMEM((CR, STRIP, CC * B), BF16),
            pltpu.VMEM((NY + 2, STRIP, CC * B), BF16),
            pltpu.VMEM((B, 256), BF16),
            pltpu.VMEM((384, B), BF16),
            pltpu.VMEM((B, (CC + 2) * B), BF16),
            dma((NZ,)),
            dma((NZ,)),
            dma((3,)),
            dma((3,)),
            dma((NY,)),
            dma((NY,)),
            dma((NY,)),
            dma((2,)),
            dma,
        ],
        compiler_params=pltpu.CompilerParams(
            collective_id=1, has_side_effects=True, vmem_limit_bytes=8 * 1024 * 1024
        ),
        name="detect",
    )(taps, pieces)


def ranks(patch):
    earlier = jnp.arange(BLK)[None, :] < jnp.arange(BLK)[:, None]
    same = patch[..., :, None] == patch[..., None, :]
    return jnp.sum((same & earlier).astype(jnp.int32), axis=-1)


def local(
    raw_blocks,
    patch_of_block,
    cell_of_block,
    band_of_block,
    block_weight,
    basis_coef,
    row_basis,
    col_basis,
    band_gain,
    filter_taps,
):
    x, z, core, y = coordinates()
    patch = patch_of_block[:, 0]
    rank = ranks(patch)
    target = band_of_block * CELLS + cell_of_block
    field = jnp.arange(4, dtype=jnp.int32)[:, None]
    names = jnp.where(field == 0, patch, jnp.where(field == 1, target, rank))
    own_details = jnp.where(field == 3, block_weight.astype(F32), names.astype(F32))
    patch_core = patch % NC
    patch_z = patch // NC % NZ
    patch_x = patch // (NC * NZ)
    slot = (patch_x * NC + patch_core) * (NY * SLOTS) + patch_z * CAP + rank
    info, slot = lax.optimization_barrier((own_details.reshape(1, 1, 4 * BLK), slot))
    outgoing = match(slot, basis_coef.astype(F32), row_basis, col_basis, raw_blocks)
    arrived, details = plane_exchange(
        outgoing.reshape(PLANE, SLOTS, STRIP, B), info
    )
    details = details.reshape(NZ, PLANE, 4, BLK)

    my_patches = (x * NZ + jnp.arange(NZ, dtype=jnp.int32)) * NC + core
    every_patch = details[:, :, 0].astype(jnp.int32).reshape(-1)
    every_target = details[:, :, 1].astype(jnp.int32).reshape(-1)
    every_weight = details[:, :, 3].reshape(-1)
    share = jnp.where(every_patch == my_patches[:, None], every_weight, 0.0).astype(BF16)
    hits = (every_target == jnp.arange(TARGETS, dtype=jnp.int32)[:, None]).astype(BF16)
    weight_sum = lax.dot_general(
        share, hits, (((1,), (1,)), ((), ())), preferred_element_type=F32
    )
    gain = (jnp.repeat(band_gain, CELLS) / jnp.maximum(weight_sum, 1.0)).reshape(-1)
    bins = (my_patches[:, None] * TARGETS + jnp.arange(TARGETS, dtype=jnp.int32)).reshape(-1)
    near = lax.dynamic_index_in_dim(details, z, axis=0, keepdims=False)
    near_names = near[:, :3].astype(jnp.int32)
    near_patch, near_target, near_rank = near_names[:, 0], near_names[:, 1], near_names[:, 2]
    near_cell = near_target % CELLS
    near_key = near_patch * TARGETS + near_target
    near_gain = jnp.sum(jnp.where(near_key[..., None] == bins, gain, 0.0), axis=-1)
    near_scale = near_gain * near[:, 3]
    chosen = (near_patch[:, None, None, :] == my_patches[:, None, None]) & (
        near_rank[:, None, None, :] == jnp.arange(CAP, dtype=jnp.int32)[:, None]
    )
    scale = jnp.sum(jnp.where(chosen, near_scale[:, None, None, :], 0.0), axis=-1).reshape(-1)
    cell = jnp.sum(jnp.where(chosen, near_cell[:, None, None, :] + 1, 0), axis=-1).reshape(-1) - 1

    pieces = gather_slots(cell, scale, arrived).reshape(NZ, CR, STRIP, CC * B)
    return detect(filter_taps, pieces)[None]


def solution(mesh):
    return jax.shard_map(
        local,
        mesh=mesh,
        in_specs=(
            P(None, ("sky", "band")),
            P(("sky", "band"), None),
            P(("sky", "band")),
            P(("sky", "band")),
            P(("sky", "band")),
            P(("sky", "band"), None),
            P(),
            P(),
            P(),
            P(),
        ),
        out_specs=P("sky", "band", None),
        check_vma=False,
    )
```
